256 devices in a mesh: dp: 16 (over z, core), fsdp: 16 (over y, x).
Axes of the slice: x: 4, y: 4, z: 8, core: 2. Of those that a mesh axis runs over, the one named last changes fastest.
Arguments:
- hidden_in: bfloat16 [2048, 2304], P(('dp', 'fsdp')), may hold values from -30 to 30
- cache_pool: bfloat16 [8448, 16, 2, 2048], P('dp', None, None, 'fsdp'), may hold values from -64 to 64
- project_in: bfloat16 [2304, 3, 2048], P('dp', None, 'fsdp'), may hold values from -0.125 to 0.125
- project_out: bfloat16 [2048, 2304], P('fsdp', 'dp'), may hold values from -0.125 to 0.125
- norm_first: bfloat16 [2304], replicated, may hold values from 0.099609375 to 1.8984375
- norm_second: bfloat16 [2304], replicated, may hold values from 0.099609375 to 1.8984375
- router: bfloat16 [2304, 8], replicated, may hold values from -0.125 to 0.125
- gate_up: bfloat16 [8, 2304, 2, 5760], P(None, 'dp', None, 'fsdp'), may hold values from -0.125 to 0.125
- expert_down: bfloat16 [8, 2304, 5760], P(None, 'dp', 'fsdp'), may hold values from -0.078125 to 0.078125
- lengths: int32 [2048], replicated, may hold values from 65 to 128, as said below
- prompt_pages: int32 [64, 4], P('dp'), may hold values from 0 to 527, as said below
- own_pages: int32 [2048, 4], P('dp'), may hold values from 0 to 527, as said below
- groups: int32 [2048], P('dp'), may hold values from 0 to 3
- move_target: int32 [16, 8], replicated, may hold values from 0 to 15, as said below
- routes: int32 [2048, 2], P(('dp', 'fsdp')), may hold values from 0 to 7, all different within a row; in each aligned block of 8 rows (0 to 7, 8 to 15, ...) at most 4 rows name the same one
Outputs:
- layer_out: bfloat16 [2048, 2304], P(('dp', 'fsdp'))
The draws below stay inside these ranges and needn't reach their ends.
Inputs may be any that keep to these rules, and one draw needn't show every extreme that they name: `lengths`: every request's cache holds its shared prompt's 4 * 16 positions and at least one more; some request holds 128. `prompt_pages`: within a row, the prompt pages of all its shared prompts and the own pages of all its requests are distinct pages. `own_pages`: within a row, the prompt pages of all its shared prompts and the own pages of all its requests are distinct pages. Row s sends its request slots 128 - 8 + j, j < 8, to rows move_target[s, j]; a row's 8 destinations are distinct and differ from s, and for each j every row is the destination of exactly one row. `routes`: in the 8 rows of one device no expert is named more than 4 times.
All inputs are finite; a program needn't handle non-finite values.
Results may differ from the reference program's by a relative error of at most 0.009.
Values may be sent and summed in bfloat16 or wider, within the bound.
A program may use at most 128 MiB of HBM per device.

```python
import math
import jax
import jax.numpy as jnp
import numpy as np
from jax import lax

D = 2304
HEADS = 32
HD = 64
FF = 5760
EXPERTS = 8
PAGE = 16
PREF = 4
OWNP = 4
GROUPS_ROW = 4
REQ_DEV = 8
CAP = 4
ROWS = 16
MIG = 8
REQ_ROW = 128
REQS = 2048
POOL = 528
LMAX = 128


def pool_layout(key):

    def one_row(row_key):
        shuffled = jax.random.permutation(row_key, POOL).astype(jnp.int32)
        prompt_part = shuffled[:GROUPS_ROW * PREF].reshape(GROUPS_ROW, PREF)
        own_part = shuffled[GROUPS_ROW * PREF:].reshape(REQ_ROW, OWNP)
        return (prompt_part, own_part)
    row_keys = jax.random.split(jax.random.fold_in(key, 11), ROWS)
    prompt_part, own_part = jax.vmap(one_row)(row_keys)
    return (prompt_part.reshape(ROWS * GROUPS_ROW, PREF), own_part.reshape(REQS, OWNP))


def draw_prompt_pages(key, part):
    return pool_layout(key)[0]


def draw_own_pages(key, part):
    return pool_layout(key)[1]


def draw_lengths(key, part):
    span_own = OWNP * PAGE
    first_draw = jax.random.randint(jax.random.fold_in(key, 1), (REQS,), 0, span_own)
    second_draw = jax.random.randint(jax.random.fold_in(key, 2), (REQS,), 0, span_own)
    extra = first_draw * second_draw // max(span_own - 1, 1)
    longest = jax.random.randint(jax.random.fold_in(key, 3), (), 0, REQS)
    result = jnp.where(jnp.arange(REQS) == longest, LMAX, PREF * PAGE + 1 + extra)
    return result.astype(jnp.int32)


def draw_move_target(key, part):
    shuffled = jax.random.permutation(jax.random.fold_in(key, 5), ROWS).astype(jnp.int32)
    offsets = jax.random.permutation(jax.random.fold_in(key, 6), ROWS - 1)[:MIG].astype(jnp.int32) + 1
    places = jnp.arange(ROWS, dtype=jnp.int32)
    targets = shuffled[(places[:, None] + offsets[None, :]) % ROWS]
    return jnp.zeros((ROWS, MIG), jnp.int32).at[shuffled].set(targets)


def draw_hidden_in(key, part):
    row_scale = jnp.exp(jax.random.uniform(jax.random.fold_in(key, 1), (REQS, 1), jnp.float32, jnp.log(0.5), jnp.log(2.0)))
    column_scale = jnp.exp(jax.random.uniform(jax.random.fold_in(key, 2), (1, D), jnp.float32, jnp.log(0.3), jnp.log(3.0)))
    base_values = jnp.clip(jax.random.normal(jax.random.fold_in(key, 3), (REQS, D), jnp.float32), -4.0, 4.0)
    return (base_values * row_scale * column_scale).astype(jnp.bfloat16)


def draw_cache_pool(key, part):
    pages_all = POOL * ROWS
    shape = (pages_all, PAGE, 2, HEADS * HD)
    result = jnp.clip(jax.random.normal(jax.random.fold_in(key, 6), shape, jnp.float32), -6.0, 6.0)
    return result.astype(jnp.bfloat16)


def place_ends(values, key, low, largest):
    longest = values.shape.index(max(values.shape))
    spots = []
    for shift in (0, 1):
        where = [jax.random.randint(jax.random.fold_in(key, axis), (), 0, length) for axis, length in enumerate(values.shape)]
        where[longest] = (where[longest] + shift) % values.shape[longest]
        spots.append(tuple(where))
    return values.at[spots[0]].set(low).at[spots[1]].set(largest)


def steps_of(rng, shape, cuts, smallest, top_value):
    def one(dim, blocks):
        heights = jax.random.uniform(jax.random.fold_in(jax.random.fold_in(rng, 6), dim), (blocks,), jnp.float32, smallest / len(cuts), top_value / len(cuts))
        return jnp.repeat(jnp.exp(heights), shape[dim] // blocks).reshape((-1,) + (1,) * (len(shape) - dim - 1))

    factor_of = one(*cuts[0])
    for cut in cuts[1:]:
        factor_of = factor_of * one(*cut)
    return factor_of


def assign_block(rng, own, number, rows, count, top, reach, skew):
    ranking = jax.random.permutation(rng, count)
    crowded, ordinary = shares(count, rows * top, reach, skew, True), shares(count, rows * top, reach, skew, False)
    places = jnp.arange(count)

    def named(sizes, rotation):
        used = int((sizes > 0).sum())
        fixed = max(1, used // 4)
        moved = fixed + (places - fixed + rotation * (used - fixed)) % max(1, count - fixed)
        return jnp.zeros((count,), jnp.int32).at[ranking[jnp.where(places < fixed, places, moved)]].set(jnp.asarray(sizes, jnp.int32))

    sizes = jnp.where(number % 4 == 0, named(crowded, number // 4), named(ordinary, number - number // 4 - 1))
    mixed = jax.random.permutation(jax.random.fold_in(own, 3), count)
    source_of, sink = mixed[0:count // 2 * 2:2], mixed[1:count // 2 * 2:2]
    room = jnp.minimum(sizes[source_of] - 1, reach - sizes[sink]) // 2
    room = jnp.where((source_of == ranking[0]) | (sink == ranking[0]) | (sizes[sink] == 0), 0, jnp.maximum(room, 0))
    moved = jax.random.randint(jax.random.fold_in(own, 4), (count // 2,), 0, 1 << 20) % (room + 1)
    sizes = sizes.at[source_of].add(-moved).at[sink].add(moved)
    items = jnp.searchsorted(jnp.cumsum(sizes), jnp.arange(rows * top), side="right").astype(jnp.int32)
    grid = items.reshape(top, rows).T
    grid = grid[jax.random.permutation(jax.random.fold_in(own, 1), rows)]
    rotation = jax.random.randint(jax.random.fold_in(own, 2), (rows, 1), 0, top)
    return jnp.take_along_axis(grid, (jnp.arange(top)[None, :] + rotation) % top, axis=1)


def shares(count, total, limit, skew, full):
    loads = [(1 << 20) // math.isqrt(standing ** skew) + 1 for standing in range(1, count + 1)]
    largest = limit if full else min(limit, max(-(-total // count), total * loads[0] // sum(loads)))
    least = 1 if total - largest >= count - 1 else 0
    holding, rest = [largest] + [least] * (count - 1), total - largest - least * (count - 1)
    while rest > 0:
        free = [i for i in range(1, count) if holding[i] < largest] or [i for i in range(1, count) if holding[i] < limit]
        whole, remaining = sum([loads[i] for i in free]), rest
        for i in free:
            addition = min(limit - holding[i], max(1, remaining * loads[i] // whole), rest)
            holding[i] = holding[i] + addition
            rest = rest - addition
    return np.array(holding)


def gaussian(rng, extent, spread, limit, pieces=(), kind=jnp.bfloat16):
    entries = jax.random.normal(rng, extent, jnp.float32) * spread
    if len(pieces) > 0:
        entries = steps_of(rng, extent, pieces, -0.22, 0.18) * entries
    return jnp.clip(entries, min=-limit, max=limit).astype(kind)


def setup_inputs(seed: int = 0) -> dict:
    key_list = jax.random.split(jax.random.key(seed), 16)
    hidden_in = draw_hidden_in(jax.random.fold_in(key_list[15], 71), 0)
    cache_pool = draw_cache_pool(jax.random.fold_in(key_list[15], 71), 0)
    project_in = gaussian(key_list[2], (D, 3, HEADS * HD), D ** -0.5, 0.125, ((0, 16), (2, 16)))
    project_out = gaussian(key_list[3], (HEADS * HD, D), (HEADS * HD) ** -0.5, 0.125, ((0, 16), (1, 16)))
    norm_first = jnp.clip(1.0 + 0.18 * jax.random.normal(key_list[4], (D,), jnp.float32), 0.099609375, 1.8984375).astype(jnp.bfloat16)
    norm_second = jnp.clip(1.0 + 0.18 * jax.random.normal(key_list[5], (D,), jnp.float32), 0.099609375, 1.8984375).astype(jnp.bfloat16)
    router = gaussian(key_list[6], (D, EXPERTS), D ** -0.5, 0.125)
    gate_up = gaussian(key_list[7], (EXPERTS, D, 2, FF), D ** -0.5, 0.125, ((1, 16), (3, 16)))
    expert_down = gaussian(key_list[8], (EXPERTS, D, FF), FF ** -0.5, 0.078125, ((1, 16), (2, 16)))
    lengths = draw_lengths(jax.random.fold_in(key_list[15], 71), 0)
    prompt_pages = draw_prompt_pages(jax.random.fold_in(key_list[15], 71), 0)
    own_pages = draw_own_pages(jax.random.fold_in(key_list[15], 71), 0)
    groups = place_ends(jax.random.randint(key_list[12], (REQS,), 0, GROUPS_ROW), jax.random.fold_in(key_list[12], 1), 0, GROUPS_ROW - 1).astype(jnp.int32)
    move_target = draw_move_target(jax.random.fold_in(key_list[15], 71), 0)
    routes_keys = jax.random.split(jax.random.fold_in(key_list[14], 1), REQS // REQ_DEV)
    routes_turns = jax.random.permutation(jax.random.fold_in(key_list[14], 3), REQS // REQ_DEV)
    routes = jax.vmap(lambda own, number: assign_block(jax.random.fold_in(key_list[14], 2), own, number, REQ_DEV, EXPERTS, 2, CAP, 1))(routes_keys, routes_turns).reshape((REQS, 2))
    return {"hidden_in": hidden_in, "cache_pool": cache_pool, "project_in": project_in, "project_out": project_out, "norm_first": norm_first, "norm_second": norm_second, "router": router, "gate_up": gate_up, "expert_down": expert_down, "lengths": lengths, "prompt_pages": prompt_pages, "own_pages": own_pages, "groups": groups, "move_target": move_target, "routes": routes}


def rms_scale(values, scaling):
    return values * lax.rsqrt(lax.optimization_barrier(jnp.mean(values * values, axis=-1, keepdims=True)) + 1e-06) * scaling.astype(jnp.float32)

def rotate(tensor, position):
    half_dim = tensor.shape[-1] // 2
    channel = jnp.arange(half_dim, dtype=jnp.float32)
    inverse = jnp.exp(-jnp.log(10000.0) * 2.0 * channel / tensor.shape[-1])
    angles = position.astype(jnp.float32)[:, None, None] * inverse
    cosine = jnp.cos(angles)
    sine_part = jnp.sin(angles)
    first_half = tensor[..., :half_dim]
    second_half = tensor[..., half_dim:]
    return jnp.concatenate([first_half * cosine - second_half * sine_part, second_half * cosine + first_half * sine_part], axis=-1)

def attend_row(query, key_new, value_new, position, page_list, cache_pool):
    count_rows = query.shape[0]
    gathered = cache_pool[page_list].astype(jnp.float32)
    gathered = gathered.reshape(count_rows, page_list.shape[1] * PAGE, 2, HEADS, HD)
    key_rows = gathered[:, :, 0]
    value_rows = gathered[:, :, 1]
    scale_factor = HD ** (-0.5)
    query_wide = query.astype(jnp.float32)
    scores = jnp.einsum('nhd,nlhd->nhl', query_wide, key_rows, precision=lax.Precision.HIGHEST) * scale_factor
    valid_mask = jnp.arange(key_rows.shape[1], dtype=jnp.int32)[None, :] < position[:, None]
    scores = jnp.where(valid_mask[:, None, :], scores, -jnp.inf)
    own_score = lax.optimization_barrier(jnp.sum(query_wide * key_new.astype(jnp.float32), axis=-1)) * scale_factor
    highest = jnp.maximum(lax.optimization_barrier(jnp.max(scores, axis=-1)), own_score)
    weights_cache = jnp.exp(scores - highest[..., None])
    weight_own = jnp.exp(own_score - highest)
    denominator = lax.optimization_barrier(jnp.sum(weights_cache, axis=-1)) + weight_own
    probs_cache = (weights_cache / denominator[..., None]).astype(jnp.bfloat16)
    prob_own = (weight_own / denominator).astype(jnp.bfloat16)
    mixture = jnp.einsum('nhl,nlhd->nhd', probs_cache.astype(jnp.float32), value_rows, precision=lax.Precision.HIGHEST)
    mixture = mixture + prob_own.astype(jnp.float32)[..., None] * value_new.astype(jnp.float32)
    return mixture.astype(jnp.bfloat16).reshape(count_rows, HEADS * HD)

def reference(hidden_in, cache_pool, project_in, project_out, norm_first, norm_second, router, gate_up, expert_down, lengths, prompt_pages, own_pages, groups, move_target, routes):
    row_ids = jnp.arange(ROWS, dtype=jnp.int32)
    matched = (move_target[:, None, :] == row_ids[None, :, None]).astype(jnp.int32)
    source_row = lax.optimization_barrier(jnp.sum(matched * row_ids[:, None, None], axis=0))
    staying = REQ_ROW - MIG
    resident = row_ids[:, None] * REQ_ROW + jnp.arange(staying, dtype=jnp.int32)[None, :]
    arrived = source_row * REQ_ROW + staying + jnp.arange(MIG, dtype=jnp.int32)[None, :]
    anchor = jnp.concatenate([resident, arrived], axis=1).reshape(REQS).astype(jnp.int32)
    old_row = jnp.arange(REQS, dtype=jnp.int32) // REQ_ROW
    prompt_list = prompt_pages[(old_row * GROUPS_ROW + groups).astype(jnp.int32)]
    page_list = jnp.concatenate([prompt_list, own_pages], axis=1) + (old_row * POOL)[:, None]
    position = lengths[anchor]
    moved = hidden_in[anchor]
    normed_attn = rms_scale(moved.astype(jnp.float32), norm_first).astype(jnp.bfloat16)
    projected = jnp.dot(normed_attn, project_in.reshape(D, 3 * HEADS * HD), preferred_element_type=jnp.float32)
    projected = projected.reshape(REQS, 3, HEADS, HD)
    query = rotate(projected[:, 0], position).astype(jnp.bfloat16)
    key_new = rotate(projected[:, 1], position).astype(jnp.bfloat16)
    value_new = projected[:, 2].astype(jnp.bfloat16)
    pages_moved = page_list[anchor]

    def blocked(array):
        return array.reshape((ROWS, REQ_ROW) + array.shape[1:])

    def one_row(item):
        return attend_row(item[0], item[1], item[2], item[3], item[4], cache_pool)
    heads_out = lax.map(one_row, (blocked(query), blocked(key_new), blocked(value_new), blocked(position), blocked(pages_moved)))
    heads_out = heads_out.reshape(REQS, HEADS * HD)
    resid = moved.astype(jnp.float32) + jnp.dot(heads_out, project_out, preferred_element_type=jnp.float32)
    moe_in = rms_scale(resid, norm_second).astype(jnp.bfloat16)
    logits = jnp.dot(moe_in, router, preferred_element_type=jnp.float32)
    chosen = jnp.take_along_axis(logits, routes, axis=1)
    route_weights = jnp.stack([jax.nn.sigmoid(chosen[:, 0] - chosen[:, 1]), jax.nn.sigmoid(chosen[:, 1] - chosen[:, 0])], axis=1)
    down_whole = jnp.transpose(expert_down, (0, 2, 1))
    capacity_all = REQS // REQ_DEV * CAP
    request_ids = jnp.arange(REQS, dtype=jnp.int32)

    def one_expert(item):
        expert, gate_expert, down_expert = item
        matches = routes == expert
        used_rows = jnp.any(matches, axis=1)
        weight_rows = lax.optimization_barrier(jnp.sum(jnp.where(matches, route_weights, 0.0), axis=1))
        ordering = jnp.argsort(jnp.where(used_rows, request_ids, REQS + request_ids))[:capacity_all].astype(jnp.int32)
        rows_in = moe_in[ordering]
        gate_part = jnp.dot(rows_in, gate_expert[:, 0], preferred_element_type=jnp.float32)
        up_part = jnp.dot(rows_in, gate_expert[:, 1], preferred_element_type=jnp.float32)
        activation = (jax.nn.silu(gate_part) * up_part).astype(jnp.bfloat16)
        expert_y = jnp.dot(activation, down_expert, preferred_element_type=jnp.float32)
        factor = weight_rows[ordering] * used_rows[ordering].astype(jnp.float32)
        return (ordering, expert_y * factor[:, None])
    orderings, contributions = lax.map(one_expert, (jnp.arange(EXPERTS, dtype=jnp.int32), gate_up, down_whole))
    moe_total = jnp.zeros((REQS, D), jnp.float32).at[orderings.reshape(-1)].add(contributions.reshape(-1, D))
    return (resid + moe_total).astype(jnp.bfloat16)
```

```python
import functools

import jax
import jax.numpy as jnp
from jax import lax
from jax.experimental import pallas as pl
from jax.experimental.pallas import tpu as pltpu
from jax.sharding import PartitionSpec as P

HD = 64
CAP = 4
LOW = -1e30
F32 = jnp.float32
BF16 = jnp.bfloat16


def vmem():
    return pl.BlockSpec(memory_space=pltpu.VMEM)


def rms_scale(values, scaling):
    return (
        values
        * lax.rsqrt(jnp.mean(values * values, axis=-1, keepdims=True) + 1e-06)
        * scaling.astype(F32)
    )


def dot_t(left, right):
    return lax.dot_general(left, right, (((1,), (1,)), ((), ())), preferred_element_type=F32)


def attention_kernel(
    page_len, tokens_ref, norm_ref, weight_ref, cos_ref, sin_ref, limit_ref, cache_ref, out_ref, wide_ref, score_ref
):
    pages = limit_ref.shape[1]
    count, width = out_ref.shape
    heads = width // HD
    wide_ref[...] = cache_ref[...].astype(F32)
    normed = rms_scale(tokens_ref[...].astype(F32), norm_ref[...]).astype(BF16)
    parts = [jnp.dot(normed, weight_ref[i], preferred_element_type=F32) for i in range(3)]
    lane = lax.broadcasted_iota(jnp.int32, (count, width), 1)
    low_half = lane % HD < HD // 2

    def rotate(values):
        partner = jnp.where(
            low_half,
            pltpu.roll(values, width - HD // 2, 1),
            pltpu.roll(values, HD // 2, 1),
        )
        return (values * cos_ref[...] + partner * sin_ref[...]).astype(BF16)

    query = rotate(parts[0])
    key_new = rotate(parts[1])
    value_new = parts[2].astype(BF16)
    head_lane = lax.broadcasted_iota(jnp.int32, (heads, count, width), 2) // HD
    head_row = lax.broadcasted_iota(jnp.int32, (heads, count, width), 0)
    wide_query = query.astype(F32)
    spread = jnp.where(head_lane == head_row, wide_query[None], 0.0)
    scale = HD ** (-0.5)
    own_score = jnp.sum(spread * key_new.astype(F32)[None], axis=-1, keepdims=True) * scale
    spread_query = spread.reshape(heads * count, width).astype(BF16)
    own_score = own_score.reshape(heads * count, 1)

    def score_step(u, highest):
        keys = wide_ref[pl.ds(2 * u, pages, stride=2 * page_len), :].astype(BF16)
        scores = dot_t(spread_query, keys) * scale
        scores = jnp.where((limit_ref[...] > u)[None], scores.reshape(heads, count, pages), LOW)
        scores = scores.reshape(heads * count, pages)
        score_ref[u] = scores
        return jnp.maximum(highest, scores)

    highest = lax.fori_loop(
        0, page_len, score_step, jnp.full((heads * count, pages), LOW, F32)
    )
    highest = jnp.maximum(jnp.max(highest, axis=-1, keepdims=True), own_score)

    def value_step(u, carry):
        total, mixture = carry
        weights = jnp.exp(score_ref[u] - highest)
        values = wide_ref[pl.ds(2 * u + 1, pages, stride=2 * page_len), :].astype(BF16)
        mixture = mixture + jnp.dot(weights.astype(BF16), values, preferred_element_type=F32)
        return total + jnp.sum(weights, axis=-1, keepdims=True), mixture

    weight_own = jnp.exp(own_score - highest)
    total, mixture = lax.fori_loop(
        0,
        page_len,
        value_step,
        (weight_own, jnp.zeros((heads * count, width), F32)),
    )
    mixture = (mixture / total).reshape(heads, count, width)
    prob_own = (weight_own / total).astype(BF16).astype(F32).reshape(heads, count, 1)
    mixture = mixture + prob_own * value_new.astype(F32)[None]
    out_ref[...] = jnp.sum(jnp.where(head_lane == head_row, mixture, 0.0), axis=0).astype(BF16)


def attention(tokens, norm, weight, position, limit, cache_pool):
    count = tokens.shape[0]
    pages, page_len, _, width = cache_pool.shape
    channel = (jnp.arange(width, dtype=jnp.int32) % (HD // 2)).astype(F32)
    inverse = jnp.exp(-jnp.log(10000.0) * 2.0 * channel / HD)
    angles = position.astype(F32)[:, None] * inverse
    sign = jnp.where(jnp.arange(width) % HD < HD // 2, -1.0, 1.0)
    rows = pages * page_len * 2
    return pl.pallas_call(
        functools.partial(attention_kernel, page_len),
        out_shape=jax.ShapeDtypeStruct((count, width), BF16),
        in_specs=[vmem()] * 7,
        out_specs=vmem(),
        scratch_shapes=[
            pltpu.VMEM((rows, width), F32),
            pltpu.VMEM((page_len, count * (width // HD), pages), F32),
        ],
        compiler_params=pltpu.CompilerParams(vmem_limit_bytes=56 * 1024 * 1024),
        name="attention",
    )(
        tokens,
        norm[None, :],
        weight,
        jnp.cos(angles),
        jnp.sin(angles) * sign,
        limit,
        cache_pool.reshape(rows, width),
    )


def local(
    hidden_in,
    cache_pool,
    project_in,
    project_out,
    norm_first,
    norm_second,
    router,
    gate_up,
    expert_down,
    lengths,
    prompt_pages,
    own_pages,
    groups,
    move_target,
    routes,
):
    rows_count = lax.axis_size("dp")
    fsdp_count = lax.axis_size("fsdp")
    my_row = lax.axis_index("dp")
    my_column = lax.axis_index("fsdp")
    req_local, model_width = hidden_in.shape
    req_row = req_local * fsdp_count
    movers = move_target.shape[1]
    staying = req_row - movers
    pages, page_len = cache_pool.shape[:2]
    head_cols = cache_pool.shape[3]
    expert_count = router.shape[1]
    rows_per_expert = rows_count // expert_count
    slots_row = (CAP + rows_per_expert - 1) // rows_per_expert
    units_here = gate_up.shape[3]
    features_here = gate_up.shape[1]

    same_core = [list(range(k, rows_count, rows_per_expert)) for k in range(rows_per_expert)]

    def spread_weights(values):
        return lax.all_to_all(
            values, "dp", split_axis=0, concat_axis=0, tiled=True, axis_index_groups=same_core
        )

    gate_half = spread_weights(jnp.transpose(gate_up, (0, 2, 1, 3)))
    down_half = spread_weights(expert_down)

    row_tokens = lax.all_gather(hidden_in, "fsdp", axis=0, tiled=True)
    weight_in = lax.all_gather(jnp.transpose(project_in, (1, 0, 2)), "dp", axis=1, tiled=True)
    weight_out = lax.all_gather(project_out.T, "dp", axis=0, tiled=True)
    group_hit = (
        groups[:, None] == jnp.arange(prompt_pages.shape[0], dtype=jnp.int32)[None, :]
    ).astype(jnp.int32)
    prompt_list = jnp.sum(group_hit[:, :, None] * prompt_pages[None, :, :], axis=1)
    page_list = jnp.concatenate([prompt_list, own_pages], axis=1)
    position = lax.dynamic_slice_in_dim(lengths, my_row * req_row, req_row)
    page_numbers = jnp.arange(pages, dtype=jnp.int32)
    limit = jnp.zeros((req_row, pages), jnp.int32)
    for j in range(page_list.shape[1]):
        valid = jnp.clip(position - page_len * j, 0, page_len)
        limit += jnp.where(page_list[:, j : j + 1] == page_numbers[None, :], valid[:, None], 0)

    heads_out = attention(row_tokens, norm_first, weight_in, position, limit, cache_pool)

    row_numbers = jnp.arange(rows_count, dtype=jnp.int32)
    send_select = (move_target[my_row][None, :] == row_numbers[:, None]).astype(BF16)
    leaving = jnp.concatenate([heads_out[staying:], row_tokens[staying:]], axis=1)
    leaving_send = jnp.dot(send_select, leaving, preferred_element_type=F32).astype(BF16)
    leaving_recv = lax.all_to_all(leaving_send, "dp", split_axis=0, concat_axis=0, tiled=True)
    arrive_select = (move_target == my_row).astype(BF16)
    arrived = lax.dot_general(
        arrive_select, leaving_recv, (((0,), (0,)), ((), ())), preferred_element_type=F32
    ).astype(BF16)
    heads_row = jnp.concatenate([heads_out[:staying], arrived[:, :head_cols]], axis=0)
    mine_tokens = jnp.where(
        my_column == fsdp_count - 1, arrived[:, head_cols:], hidden_in
    )
    partial_out = dot_t(heads_row, weight_out).astype(BF16)
    partial_recv = lax.all_to_all(
        partial_out.reshape(fsdp_count, req_local, model_width),
        "fsdp",
        split_axis=0,
        concat_axis=0,
        tiled=True,
    )
    attn_proj = jnp.sum(partial_recv.astype(F32), axis=0)
    resid = mine_tokens.astype(F32) + attn_proj
    moe_in = rms_scale(resid, norm_second).astype(BF16)
    logits = jnp.dot(moe_in, router, preferred_element_type=F32)
    expert_ids = jnp.arange(expert_count, dtype=jnp.int32)
    picked = routes[:, :, None] == expert_ids[None, None, :]
    chosen = jnp.sum(jnp.where(picked, logits[:, None, :], 0.0), axis=-1)
    weight_pair = jnp.stack(
        [jax.nn.sigmoid(chosen[:, 0] - chosen[:, 1]), jax.nn.sigmoid(chosen[:, 1] - chosen[:, 0])],
        axis=1,
    )
    mix_expert = jnp.sum(picked.astype(F32) * weight_pair[:, :, None], axis=1)
    member = jnp.sum(picked.astype(jnp.int32), axis=1)
    rank_expert = jnp.cumsum(member, axis=0) - member
    expert_of_row = (row_numbers[:, None] // rows_per_expert == expert_ids[None, :]).astype(
        jnp.int32
    )
    replica_of_row = row_numbers % rows_per_expert
    member_row = jnp.sum(member[:, None, :] * expert_of_row[None, :, :], axis=-1)
    rank_row = jnp.sum(rank_expert[:, None, :] * expert_of_row[None, :, :], axis=-1)
    mix_row = jnp.sum(mix_expert[:, None, :] * expert_of_row[None, :, :].astype(F32), axis=-1)
    slot_ids = jnp.arange(slots_row, dtype=jnp.int32)
    wanted_rank = slot_ids[None, :, None] * rows_per_expert + replica_of_row[:, None, None]
    select = (member_row.T[:, None, :] == 1) & (rank_row.T[:, None, :] == wanted_rank)
    dispatch = jnp.einsum(
        "dst,tm->dsm", select.astype(BF16), moe_in, preferred_element_type=F32
    ).astype(BF16)
    received = lax.all_to_all(dispatch, "dp", split_axis=0, concat_axis=0, tiled=True)
    expert_tokens = lax.all_gather(received[None], "fsdp", axis=0, tiled=True)
    flattened = expert_tokens.reshape(-1, model_width)

    swap = [(d, d ^ 1) for d in range(rows_count)]
    first_core = my_row % 2 == 0

    def both(values):
        other = lax.ppermute(values, "dp", swap)
        return jnp.stack(
            [jnp.where(first_core, values, other), jnp.where(first_core, other, values)], axis=1
        )

    gate_whole = both(gate_half)
    down_whole = both(down_half)
    down_cols = down_whole.reshape(model_width, units_here)
    gate_cols = gate_whole[:, :, 0].reshape(model_width, units_here)
    up_cols = gate_whole[:, :, 1].reshape(model_width, units_here)
    gate_part = jnp.dot(flattened, gate_cols, preferred_element_type=F32)
    up_part = jnp.dot(flattened, up_cols, preferred_element_type=F32)
    activation = (jax.nn.silu(gate_part) * up_part).astype(BF16)
    expert_y = dot_t(activation, down_cols).astype(BF16)
    returned = lax.all_to_all(
        expert_y.reshape(fsdp_count, rows_count * slots_row, model_width),
        "fsdp",
        split_axis=0,
        concat_axis=0,
        tiled=True,
    )
    returned = jnp.sum(returned.astype(F32), axis=0).astype(BF16)
    back_rows = lax.all_to_all(
        returned.reshape(rows_count, slots_row, model_width),
        "dp",
        split_axis=0,
        concat_axis=0,
        tiled=True,
    )
    coefficient = select.astype(F32) * mix_row.T[:, None, :]
    moe_total = jnp.einsum(
        "dst,dsm->tm", coefficient, back_rows.astype(F32), precision=lax.Precision.HIGHEST
    )
    return (resid + moe_total).astype(BF16)


def solution(mesh):
    placed = (
        P(("dp", "fsdp"), None),
        P("dp", None, None, "fsdp"),
        P("dp", None, "fsdp"),
        P("fsdp", "dp"),
        P(),
        P(),
        P(),
        P(None, "dp", None, "fsdp"),
        P(None, "dp", "fsdp"),
        P(),
        P("dp", None),
        P("dp", None),
        P("dp"),
        P(),
        P(("dp", "fsdp"), None),
    )
    return jax.shard_map(
        local, mesh=mesh, in_specs=placed, out_specs=P(("dp", "fsdp"), None), check_vma=False
    )
```

```python
import functools

import jax
import jax.numpy as jnp
from jax import lax
from jax.experimental import pallas as pl
from jax.experimental.pallas import tpu as pltpu
from jax.sharding import PartitionSpec as P

HD = 64
CAP = 4
LOW = -1e30
F32 = jnp.float32
BF16 = jnp.bfloat16


def vmem():
    return pl.BlockSpec(memory_space=pltpu.VMEM)


def rms_scale(values, scaling):
    return (
        values
        * lax.rsqrt(jnp.mean(values * values, axis=-1, keepdims=True) + 1e-06)
        * scaling.astype(F32)
    )


def dot_t(left, right):
    return lax.dot_general(left, right, (((1,), (1,)), ((), ())), preferred_element_type=F32)


def attention_kernel(
    page_len, tokens_ref, norm_ref, weight_ref, cos_ref, sin_ref, limit_ref, cache_ref, out_ref, wide_ref, score_ref
):
    pages = limit_ref.shape[1]
    count, width = out_ref.shape
    heads = width // HD
    wide_ref[...] = cache_ref[...].astype(F32)
    normed = rms_scale(tokens_ref[...].astype(F32), norm_ref[...]).astype(BF16)
    parts = [jnp.dot(normed, weight_ref[i], preferred_element_type=F32) for i in range(3)]
    lane = lax.broadcasted_iota(jnp.int32, (count, width), 1)
    low_half = lane % HD < HD // 2

    def rotate(values):
        partner = jnp.where(
            low_half,
            pltpu.roll(values, width - HD // 2, 1),
            pltpu.roll(values, HD // 2, 1),
        )
        return (values * cos_ref[...] + partner * sin_ref[...]).astype(BF16)

    query = rotate(parts[0])
    key_new = rotate(parts[1])
    value_new = parts[2].astype(BF16)
    head_lane = lax.broadcasted_iota(jnp.int32, (heads, count, width), 2) // HD
    head_row = lax.broadcasted_iota(jnp.int32, (heads, count, width), 0)
    wide_query = query.astype(F32)
    spread = jnp.where(head_lane == head_row, wide_query[None], 0.0)
    scale = HD ** (-0.5)
    own_score = jnp.sum(spread * key_new.astype(F32)[None], axis=-1, keepdims=True) * scale
    spread_query = spread.reshape(heads * count, width).astype(BF16)
    own_score = own_score.reshape(heads * count, 1)

    def score_step(u, highest):
        keys = wide_ref[pl.ds(2 * u, pages, stride=2 * page_len), :].astype(BF16)
        scores = dot_t(spread_query, keys) * scale
        scores = jnp.where((limit_ref[...] > u)[None], scores.reshape(heads, count, pages), LOW)
        scores = scores.reshape(heads * count, pages)
        score_ref[u] = scores
        return jnp.maximum(highest, scores)

    highest = lax.fori_loop(
        0, page_len, score_step, jnp.full((heads * count, pages), LOW, F32)
    )
    highest = jnp.maximum(jnp.max(highest, axis=-1, keepdims=True), own_score)

    def value_step(u, carry):
        total, mixture = carry
        weights = jnp.exp(score_ref[u] - highest)
        values = wide_ref[pl.ds(2 * u + 1, pages, stride=2 * page_len), :].astype(BF16)
        mixture = mixture + jnp.dot(weights.astype(BF16), values, preferred_element_type=F32)
        return total + jnp.sum(weights, axis=-1, keepdims=True), mixture

    weight_own = jnp.exp(own_score - highest)
    total, mixture = lax.fori_loop(
        0,
        page_len,
        value_step,
        (weight_own, jnp.zeros((heads * count, width), F32)),
    )
    mixture = (mixture / total).reshape(heads, count, width)
    prob_own = (weight_own / total).astype(BF16).astype(F32).reshape(heads, count, 1)
    mixture = mixture + prob_own * value_new.astype(F32)[None]
    out_ref[...] = jnp.sum(jnp.where(head_lane == head_row, mixture, 0.0), axis=0).astype(BF16)


def attention(tokens, norm, weight, position, limit, cache_pool):
    count = tokens.shape[0]
    pages, page_len, _, width = cache_pool.shape
    channel = (jnp.arange(width, dtype=jnp.int32) % (HD // 2)).astype(F32)
    inverse = jnp.exp(-jnp.log(10000.0) * 2.0 * channel / HD)
    angles = position.astype(F32)[:, None] * inverse
    sign = jnp.where(jnp.arange(width) % HD < HD // 2, -1.0, 1.0)
    rows = pages * page_len * 2
    return pl.pallas_call(
        functools.partial(attention_kernel, page_len),
        out_shape=jax.ShapeDtypeStruct((count, width), BF16),
        in_specs=[vmem()] * 7,
        out_specs=vmem(),
        scratch_shapes=[
            pltpu.VMEM((rows, width), F32),
            pltpu.VMEM((page_len, count * (width // HD), pages), F32),
        ],
        compiler_params=pltpu.CompilerParams(vmem_limit_bytes=56 * 1024 * 1024),
        name="attention",
    )(
        tokens,
        norm[None, :],
        weight,
        jnp.cos(angles),
        jnp.sin(angles) * sign,
        limit,
        cache_pool.reshape(rows, width),
    )


def exchange_kernel(axis, count, gather, reduce, src_ref, out_ref, *scratch):
    land_ref = scratch[0] if reduce else out_ref
    send_sem, recv_sem, own_sem = scratch[-3:]
    me = lax.axis_index(axis)
    barrier = pltpu.get_barrier_semaphore()
    for step in range(1, count):
        pl.semaphore_signal(
            barrier,
            inc=1,
            device_id={axis: lax.rem(me + step, count)},
            device_id_type=pl.DeviceIdType.MESH,
        )
    pl.semaphore_wait(barrier, count - 1)
    copies = []
    for step in range(1, count):
        peer = lax.rem(me + step, count)
        copy = pltpu.make_async_remote_copy(
            src_ref=src_ref if gather else src_ref.at[peer],
            dst_ref=land_ref.at[me],
            send_sem=send_sem.at[step],
            recv_sem=recv_sem.at[step],
            device_id={axis: peer},
            device_id_type=pl.DeviceIdType.MESH,
        )
        copy.start()
        copies.append(copy)
    own = pltpu.make_async_copy(src_ref if gather else src_ref.at[me], land_ref.at[me], own_sem)
    own.start()
    own.wait()
    for copy in copies:
        copy.wait()
    if reduce:
        width = land_ref.shape[2]
        block = width // 6
        for start in range(0, width, block):
            total = land_ref[0, :, start : start + block].astype(F32)
            for source in range(1, count):
                total = total + land_ref[source, :, start : start + block].astype(F32)
            out_ref[:, start : start + block] = total.astype(out_ref.dtype)


def exchange(values, axis, number, name, gather=False, reduce=None):
    count = lax.axis_size(axis)
    block = values.shape if gather else values.shape[1:]
    landing = (count,) + block
    semaphores = [
        pltpu.SemaphoreType.DMA((count,)),
        pltpu.SemaphoreType.DMA((count,)),
        pltpu.SemaphoreType.DMA,
    ]
    if reduce is None:
        result = jax.ShapeDtypeStruct(landing, values.dtype)
        scratch = semaphores
    else:
        result = jax.ShapeDtypeStruct(block, reduce)
        scratch = [pltpu.VMEM(landing, values.dtype)] + semaphores
    return pl.pallas_call(
        functools.partial(exchange_kernel, axis, count, gather, reduce is not None),
        out_shape=result,
        in_specs=[vmem()],
        out_specs=vmem(),
        scratch_shapes=scratch,
        compiler_params=pltpu.CompilerParams(collective_id=number, has_side_effects=True),
        name=name,
    )(values)


def local(
    hidden_in,
    cache_pool,
    project_in,
    project_out,
    norm_first,
    norm_second,
    router,
    gate_up,
    expert_down,
    lengths,
    prompt_pages,
    own_pages,
    groups,
    move_target,
    routes,
):
    rows_count = lax.axis_size("dp")
    fsdp_count = lax.axis_size("fsdp")
    my_row = lax.axis_index("dp")
    my_column = lax.axis_index("fsdp")
    req_local, model_width = hidden_in.shape
    req_row = req_local * fsdp_count
    movers = move_target.shape[1]
    staying = req_row - movers
    pages, page_len = cache_pool.shape[:2]
    head_cols = cache_pool.shape[3]
    expert_count = router.shape[1]
    rows_per_expert = rows_count // expert_count
    slots_row = (CAP + rows_per_expert - 1) // rows_per_expert
    units_here = gate_up.shape[3]
    features_here = gate_up.shape[1]

    same_core = [list(range(k, rows_count, rows_per_expert)) for k in range(rows_per_expert)]

    def spread_weights(values):
        return lax.all_to_all(
            values, "dp", split_axis=0, concat_axis=0, tiled=True, axis_index_groups=same_core
        )

    row_tokens = exchange(hidden_in, "fsdp", 0, "row_tokens", gather=True)
    row_tokens = row_tokens.reshape(req_row, model_width)
    weights = jnp.concatenate(
        [jnp.transpose(project_in, (1, 0, 2)), project_out.T[None]], axis=0
    )
    weights = lax.all_gather(weights, "dp", axis=1, tiled=True)
    weight_in, weight_out = weights[:3], weights[3]
    gate_up, expert_down, weights = lax.optimization_barrier((gate_up, expert_down, weights))
    gate_own = spread_weights(
        gate_up.reshape(expert_count, features_here, 2 * units_here)
    ).reshape(-1, 2 * units_here)
    down_own = spread_weights(expert_down).reshape(-1, units_here)
    swap = [(d, d ^ 1) for d in range(rows_count)]
    gate_other = lax.ppermute(gate_own, "dp", swap)
    down_other = lax.ppermute(down_own, "dp", swap)

    group_hit = (
        groups[:, None] == jnp.arange(prompt_pages.shape[0], dtype=jnp.int32)[None, :]
    ).astype(jnp.int32)
    prompt_list = jnp.sum(group_hit[:, :, None] * prompt_pages[None, :, :], axis=1)
    page_list = jnp.concatenate([prompt_list, own_pages], axis=1)
    position = lax.dynamic_slice_in_dim(lengths, my_row * req_row, req_row)
    page_numbers = jnp.arange(pages, dtype=jnp.int32)
    limit = jnp.zeros((req_row, pages), jnp.int32)
    for j in range(page_list.shape[1]):
        valid = jnp.clip(position - page_len * j, 0, page_len)
        limit += jnp.where(page_list[:, j : j + 1] == page_numbers[None, :], valid[:, None], 0)

    heads_out = attention(row_tokens, norm_first, weight_in, position, limit, cache_pool)

    row_numbers = jnp.arange(rows_count, dtype=jnp.int32)
    send_select = (move_target[my_row][None, :] == row_numbers[:, None]).astype(BF16)
    leaving = jnp.concatenate([heads_out[staying:], row_tokens[staying:]], axis=1)
    leaving_send = jnp.dot(send_select, leaving, preferred_element_type=F32).astype(BF16)
    leaving_recv = exchange(leaving_send[:, None, :], "dp", 1, "leaving")[:, 0]
    arrive_select = (move_target == my_row).astype(BF16)
    arrived = lax.dot_general(
        arrive_select, leaving_recv, (((0,), (0,)), ((), ())), preferred_element_type=F32
    ).astype(BF16)
    heads_row = jnp.concatenate([heads_out[:staying], arrived[:, :head_cols]], axis=0)
    mine_tokens = jnp.where(
        my_column == fsdp_count - 1, arrived[:, head_cols:], hidden_in
    )
    partial_out = dot_t(heads_row, weight_out).astype(BF16)
    attn_proj = exchange(
        partial_out.reshape(fsdp_count, req_local, model_width),
        "fsdp",
        2,
        "partial_out",
        reduce=F32,
    )
    resid = mine_tokens.astype(F32) + attn_proj
    moe_in = rms_scale(resid, norm_second).astype(BF16)
    logits = jnp.dot(moe_in, router, preferred_element_type=F32)
    expert_ids = jnp.arange(expert_count, dtype=jnp.int32)
    picked = routes[:, :, None] == expert_ids[None, None, :]
    chosen = jnp.sum(jnp.where(picked, logits[:, None, :], 0.0), axis=-1)
    weight_pair = jnp.stack(
        [jax.nn.sigmoid(chosen[:, 0] - chosen[:, 1]), jax.nn.sigmoid(chosen[:, 1] - chosen[:, 0])],
        axis=1,
    )
    mix_expert = jnp.sum(picked.astype(F32) * weight_pair[:, :, None], axis=1)
    member = jnp.sum(picked.astype(jnp.int32), axis=1)
    rank_expert = jnp.cumsum(member, axis=0) - member
    expert_of_row = (row_numbers[:, None] // rows_per_expert == expert_ids[None, :]).astype(
        jnp.int32
    )
    replica_of_row = row_numbers % rows_per_expert
    member_row = jnp.sum(member[:, None, :] * expert_of_row[None, :, :], axis=-1)
    rank_row = jnp.sum(rank_expert[:, None, :] * expert_of_row[None, :, :], axis=-1)
    mix_row = jnp.sum(mix_expert[:, None, :] * expert_of_row[None, :, :].astype(F32), axis=-1)
    slot_ids = jnp.arange(slots_row, dtype=jnp.int32)
    wanted_rank = slot_ids[None, :, None] * rows_per_expert + replica_of_row[:, None, None]
    select = (member_row.T[:, None, :] == 1) & (rank_row.T[:, None, :] == wanted_rank)
    dispatch = jnp.einsum(
        "dst,tm->dsm", select.astype(BF16), moe_in, preferred_element_type=F32
    ).astype(BF16)
    by_core = dispatch.reshape(rows_count // 2, 2, slots_row, rows_count // 2, 2, features_here)
    half = model_width // 2
    cores = [by_core[:, :, :, :, c].reshape(rows_count // 2, 2, slots_row, half) for c in range(2)]
    dispatch = jnp.stack(
        [
            jnp.concatenate([cores[0][:, 0], cores[1][:, 0]], axis=-1),
            jnp.concatenate([cores[1][:, 1], cores[0][:, 1]], axis=-1),
        ],
        axis=1,
    ).reshape(rows_count, slots_row, model_width)
    received = exchange(dispatch, "dp", 3, "dispatch")
    expert_tokens = exchange(
        received.reshape(rows_count * slots_row, model_width), "fsdp", 4, "expert_tokens", gather=True
    )
    flattened = expert_tokens.reshape(-1, model_width)
    gate_up_part = jnp.dot(
        flattened[:, :half], gate_own, preferred_element_type=F32
    ) + jnp.dot(flattened[:, half:], gate_other, preferred_element_type=F32)
    activation = (
        jax.nn.silu(gate_up_part[:, :units_here]) * gate_up_part[:, units_here:]
    ).astype(BF16)
    expert_y = jnp.concatenate(
        [dot_t(activation, down_own).astype(BF16), dot_t(activation, down_other).astype(BF16)],
        axis=1,
    )
    returned = exchange(
        expert_y.reshape(fsdp_count, rows_count * slots_row, model_width),
        "fsdp",
        5,
        "expert_sums",
        reduce=BF16,
    )
    back_rows = exchange(
        returned.reshape(rows_count, slots_row, model_width), "dp", 6, "back_rows"
    )
    coefficient = select.astype(F32) * mix_row.T[:, None, :]
    coefficient = coefficient.reshape(rows_count // 2, 2, slots_row, req_local)
    back_rows = back_rows.astype(F32).reshape(rows_count // 2, 2, slots_row, model_width)
    sums = [
        jnp.einsum(
            "dst,dsm->tm", coefficient[:, c], back_rows[:, c], precision=lax.Precision.HIGHEST
        )
        for c in range(2)
    ]
    by_core = [
        sums[0][:, :half] + sums[1][:, half:],
        sums[0][:, half:] + sums[1][:, :half],
    ]
    moe_total = jnp.stack(
        [part.reshape(req_local, rows_count // 2, features_here) for part in by_core], axis=2
    ).reshape(req_local, model_width)
    return (resid + moe_total).astype(BF16)


def solution(mesh):
    placed = (
        P(("dp", "fsdp"), None),
        P("dp", None, None, "fsdp"),
        P("dp", None, "fsdp"),
        P("fsdp", "dp"),
        P(),
        P(),
        P(),
        P(None, "dp", None, "fsdp"),
        P(None, "dp", "fsdp"),
        P(),
        P("dp", None),
        P("dp", None),
        P("dp"),
        P(),
        P(("dp", "fsdp"), None),
    )
    return jax.shard_map(
        local, mesh=mesh, in_specs=placed, out_specs=P(("dp", "fsdp"), None), check_vma=False
    )
```

```python
import functools

import jax
import jax.numpy as jnp
from jax import lax
from jax.experimental import pallas as pl
from jax.experimental.pallas import tpu as pltpu
from jax.sharding import PartitionSpec as P

HD = 64
CAP = 4
LOW = -1e30
F32 = jnp.float32
BF16 = jnp.bfloat16


def vmem():
    return pl.BlockSpec(memory_space=pltpu.VMEM)


def rms_scale(values, scaling):
    return (
        values
        * lax.rsqrt(jnp.mean(values * values, axis=-1, keepdims=True) + 1e-06)
        * scaling.astype(F32)
    )


def dot_t(left, right):
    return lax.dot_general(left, right, (((1,), (1,)), ((), ())), preferred_element_type=F32)


def attention_kernel(
    page_len, tokens_ref, norm_ref, weight_ref, cos_ref, sin_ref, limit_ref, cache_ref, out_ref, wide_ref, score_ref
):
    pages = limit_ref.shape[1]
    count, width = out_ref.shape
    heads = width // HD
    wide_ref[...] = cache_ref[...].astype(F32)
    normed = rms_scale(tokens_ref[...].astype(F32), norm_ref[...]).astype(BF16)
    parts = [jnp.dot(normed, weight_ref[i], preferred_element_type=F32) for i in range(3)]
    lane = lax.broadcasted_iota(jnp.int32, (count, width), 1)
    low_half = lane % HD < HD // 2

    def rotate(values):
        partner = jnp.where(
            low_half,
            pltpu.roll(values, width - HD // 2, 1),
            pltpu.roll(values, HD // 2, 1),
        )
        return (values * cos_ref[...] + partner * sin_ref[...]).astype(BF16)

    query = rotate(parts[0])
    key_new = rotate(parts[1])
    value_new = parts[2].astype(BF16)
    head_lane = lax.broadcasted_iota(jnp.int32, (heads, count, width), 2) // HD
    head_row = lax.broadcasted_iota(jnp.int32, (heads, count, width), 0)
    wide_query = query.astype(F32)
    spread = jnp.where(head_lane == head_row, wide_query[None], 0.0)
    scale = HD ** (-0.5)
    own_score = jnp.sum(spread * key_new.astype(F32)[None], axis=-1, keepdims=True) * scale
    spread_query = spread.reshape(heads * count, width).astype(BF16)
    own_score = own_score.reshape(heads * count, 1)

    def score_step(u, highest):
        keys = wide_ref[pl.ds(2 * u, pages, stride=2 * page_len), :].astype(BF16)
        scores = dot_t(spread_query, keys) * scale
        scores = jnp.where((limit_ref[...] > u)[None], scores.reshape(heads, count, pages), LOW)
        scores = scores.reshape(heads * count, pages)
        score_ref[u] = scores
        return jnp.maximum(highest, scores)

    highest = lax.fori_loop(
        0, page_len, score_step, jnp.full((heads * count, pages), LOW, F32)
    )
    highest = jnp.maximum(jnp.max(highest, axis=-1, keepdims=True), own_score)

    def value_step(u, carry):
        total, mixture = carry
        weights = jnp.exp(score_ref[u] - highest)
        values = wide_ref[pl.ds(2 * u + 1, pages, stride=2 * page_len), :].astype(BF16)
        mixture = mixture + jnp.dot(weights.astype(BF16), values, preferred_element_type=F32)
        return total + jnp.sum(weights, axis=-1, keepdims=True), mixture

    weight_own = jnp.exp(own_score - highest)
    total, mixture = lax.fori_loop(
        0,
        page_len,
        value_step,
        (weight_own, jnp.zeros((heads * count, width), F32)),
    )
    mixture = (mixture / total).reshape(heads, count, width)
    prob_own = (weight_own / total).astype(BF16).astype(F32).reshape(heads, count, 1)
    mixture = mixture + prob_own * value_new.astype(F32)[None]
    out_ref[...] = jnp.sum(jnp.where(head_lane == head_row, mixture, 0.0), axis=0).astype(BF16)


def attention(tokens, norm, weight, position, limit, cache_pool):
    count = tokens.shape[0]
    pages, page_len, _, width = cache_pool.shape
    channel = (jnp.arange(width, dtype=jnp.int32) % (HD // 2)).astype(F32)
    inverse = jnp.exp(-jnp.log(10000.0) * 2.0 * channel / HD)
    angles = position.astype(F32)[:, None] * inverse
    sign = jnp.where(jnp.arange(width) % HD < HD // 2, -1.0, 1.0)
    rows = pages * page_len * 2
    return pl.pallas_call(
        functools.partial(attention_kernel, page_len),
        out_shape=jax.ShapeDtypeStruct((count, width), BF16),
        in_specs=[vmem()] * 7,
        out_specs=vmem(),
        scratch_shapes=[
            pltpu.VMEM((rows, width), F32),
            pltpu.VMEM((page_len, count * (width // HD), pages), F32),
        ],
        compiler_params=pltpu.CompilerParams(vmem_limit_bytes=56 * 1024 * 1024),
        cost_estimate=pl.CostEstimate(
            flops=4 * count * width * rows, bytes_accessed=60_000_000, transcendentals=0
        ),
        name="attention",
    )(
        tokens,
        norm[None, :],
        weight,
        jnp.cos(angles),
        jnp.sin(angles) * sign,
        limit,
        cache_pool.reshape(rows, width),
    )


def exchange_kernel(axis, count, gather, reduce, src_ref, out_ref, *scratch):
    land_ref = scratch[0] if reduce else out_ref
    send_sem, recv_sem, own_sem = scratch[-3:]
    me = lax.axis_index(axis)
    barrier = pltpu.get_barrier_semaphore()
    for step in range(1, count):
        pl.semaphore_signal(
            barrier,
            inc=1,
            device_id={axis: lax.rem(me + step, count)},
            device_id_type=pl.DeviceIdType.MESH,
        )
    pl.semaphore_wait(barrier, count - 1)
    copies = []
    for step in range(1, count):
        peer = lax.rem(me + step, count)
        copy = pltpu.make_async_remote_copy(
            src_ref=src_ref if gather else src_ref.at[peer],
            dst_ref=land_ref.at[me],
            send_sem=send_sem.at[step],
            recv_sem=recv_sem.at[step],
            device_id={axis: peer},
            device_id_type=pl.DeviceIdType.MESH,
        )
        copy.start()
        copies.append(copy)
    own = pltpu.make_async_copy(src_ref if gather else src_ref.at[me], land_ref.at[me], own_sem)
    own.start()
    own.wait()
    for copy in copies:
        copy.wait()
    if reduce:
        width = land_ref.shape[2]
        block = width // 6
        for start in range(0, width, block):
            total = land_ref[0, :, start : start + block].astype(F32)
            for source in range(1, count):
                total = total + land_ref[source, :, start : start + block].astype(F32)
            out_ref[:, start : start + block] = total.astype(out_ref.dtype)


def exchange(values, axis, number, name, gather=False, reduce=None):
    count = lax.axis_size(axis)
    block = values.shape if gather else values.shape[1:]
    landing = (count,) + block
    semaphores = [
        pltpu.SemaphoreType.DMA((count,)),
        pltpu.SemaphoreType.DMA((count,)),
        pltpu.SemaphoreType.DMA,
    ]
    if reduce is None:
        result = jax.ShapeDtypeStruct(landing, values.dtype)
        scratch = semaphores
    else:
        result = jax.ShapeDtypeStruct(block, reduce)
        scratch = [pltpu.VMEM(landing, values.dtype)] + semaphores
    return pl.pallas_call(
        functools.partial(exchange_kernel, axis, count, gather, reduce is not None),
        out_shape=result,
        in_specs=[vmem()],
        out_specs=vmem(),
        scratch_shapes=scratch,
        compiler_params=pltpu.CompilerParams(collective_id=number, has_side_effects=True),
        cost_estimate=pl.CostEstimate(flops=0, bytes_accessed=200_000_000, transcendentals=0),
        name=name,
    )(values)


def torus_ids(axis, side):
    me = lax.axis_index(axis)
    y, x = me // side, lax.rem(me, side)

    def peer(along_y, step):
        if along_y:
            return {axis: lax.rem(y + step, side) * side + x}
        return {axis: y * side + lax.rem(x + step, side)}

    return y, x, peer


def torus_barrier(peer, side):
    barrier = pltpu.get_barrier_semaphore()
    for along_y in (False, True):
        for step in range(1, side):
            pl.semaphore_signal(
                barrier,
                inc=1,
                device_id=peer(along_y, step),
                device_id_type=pl.DeviceIdType.MESH,
            )
    pl.semaphore_wait(barrier, 2 * (side - 1))


def torus_gather_kernel(axis, side, src_ref, out_ref, send_sem, recv_sem, own_sem):
    y, x, peer = torus_ids(axis, side)
    half = src_ref.shape[0] // 2
    rows = [pl.ds(0, half), pl.ds(half, half)]
    part = [pl.ds(0, side // 2), pl.ds(side // 2, side - side // 2)]
    torus_barrier(peer, side)

    def send(h, number, src, dst, device):
        copy = pltpu.make_async_remote_copy(
            src_ref=src,
            dst_ref=dst,
            send_sem=send_sem.at[h, number],
            recv_sem=recv_sem.at[h, number],
            device_id=device,
            device_id_type=pl.DeviceIdType.MESH,
        )
        copy.start()
        return copy

    first = [
        [
            send(h, step - 1, src_ref.at[rows[h]], out_ref.at[y, x, rows[h]], peer(h == 1, step))
            for step in range(1, side)
        ]
        for h in range(2)
    ]
    own = pltpu.make_async_copy(src_ref, out_ref.at[y, x], own_sem)
    own.start()
    own.wait()

    def group(h, step, blocks):
        if h == 0:
            return out_ref.at[lax.rem(y + step, side), blocks, rows[h]]
        return out_ref.at[blocks, lax.rem(x + step, side), rows[h]]

    whole = pl.ds(0, side)
    second = []
    for h in range(2):
        for copy in first[h]:
            copy.wait()
        second.append(
            [
                send(h, 3, group(h, 0, whole), group(h, 0, whole), peer(h == 0, 1)),
                send(h, 4, group(h, 0, whole), group(h, 0, whole), peer(h == 0, side - 1)),
            ]
        )
    third = []
    for h in range(2):
        for k, back in ((0, side - 1), (1, 1)):
            second[h][k].wait()
            source = group(h, back, part[k])
            third.append(send(h, 5 + k, source, source, peer(h == 0, side - back)))
    for copy in third:
        copy.wait()


def torus_gather(values, axis, number, name):
    count = lax.axis_size(axis)
    side = 4
    return pl.pallas_call(
        functools.partial(torus_gather_kernel, axis, side),
        out_shape=jax.ShapeDtypeStruct((side, count // side) + values.shape, values.dtype),
        in_specs=[vmem()],
        out_specs=vmem(),
        scratch_shapes=[
            pltpu.SemaphoreType.DMA((2, 7)),
            pltpu.SemaphoreType.DMA((2, 7)),
            pltpu.SemaphoreType.DMA,
        ],
        compiler_params=pltpu.CompilerParams(collective_id=number, has_side_effects=True),
        cost_estimate=pl.CostEstimate(flops=0, bytes_accessed=60_000_000, transcendentals=0),
        name=name,
    )(values)


def torus_sum_kernel(
    axis, side, src_ref, out_ref, land_ref, relay_ref, sum_ref, last_ref, send_sem, recv_sem
):
    y, x, peer = torus_ids(axis, side)
    half = src_ref.shape[2] // 2
    width = src_ref.shape[3]
    block = width // 3
    rows = [pl.ds(0, half), pl.ds(half, half)]
    part = [pl.ds(0, side // 2), pl.ds(side // 2, side - side // 2)]
    whole = pl.ds(0, side)
    torus_barrier(peer, side)

    def send(h, number, src, dst, device):
        copy = pltpu.make_async_remote_copy(
            src_ref=src,
            dst_ref=dst,
            send_sem=send_sem.at[h, number],
            recv_sem=recv_sem.at[h, number],
            device_id=device,
            device_id_type=pl.DeviceIdType.MESH,
        )
        copy.start()
        return copy

    def terms(h, step, blocks):
        if h == 0:
            return src_ref.at[blocks, lax.rem(x + step, side), rows[h]]
        return src_ref.at[lax.rem(y + step, side), blocks, rows[h]]

    far, near, relays = [], [], []
    for h in range(2):
        far.append(
            [
                send(h, 0, terms(h, 2, part[0]), relay_ref.at[h, 0], peer(h == 1, 1)),
                send(h, 1, terms(h, 2, part[1]), relay_ref.at[h, 1], peer(h == 1, side - 1)),
            ]
        )
    for h in range(2):
        near.append(
            [
                send(h, 2, terms(h, 1, whole), land_ref.at[h, 0], peer(h == 1, 1)),
                send(h, 3, terms(h, side - 1, whole), land_ref.at[h, 2], peer(h == 1, side - 1)),
            ]
        )
    for h in range(2):
        for k, step in ((0, 1), (1, side - 1)):
            far[h][k].wait()
            relays.append(
                send(
                    h, 4 + k, relay_ref.at[h, k], land_ref.at[h, 1, part[k]], peer(h == 1, step)
                )
            )
    for h in range(2):
        for copy in near[h]:
            copy.wait()
    for copy in relays:
        copy.wait()
    last = []
    for h in range(2):
        for b in range(side):
            for start in range(0, width, block):
                cols = slice(start, start + block)
                if h == 0:
                    total = src_ref[b, x, 0:half, cols].astype(F32)
                else:
                    total = src_ref[y, b, half : 2 * half, cols].astype(F32)
                for k in range(side - 1):
                    total = total + land_ref[h, k, b, :, cols].astype(F32)
                sum_ref[h, b, :, cols] = total.astype(sum_ref.dtype)
        mine = y if h == 0 else x
        for step in range(1, side):
            last.append(
                send(
                    h,
                    5 + step,
                    sum_ref.at[h, lax.rem(mine + step, side)],
                    last_ref.at[h, step - 1],
                    peer(h == 0, step),
                )
            )
    for copy in last:
        copy.wait()
    for h in range(2):
        mine = y if h == 0 else x
        for start in range(0, width, block):
            cols = slice(start, start + block)
            total = sum_ref[h, mine, :, cols].astype(F32)
            for k in range(side - 1):
                total = total + last_ref[h, k, :, cols].astype(F32)
            out_ref[h * half : (h + 1) * half, cols] = total.astype(out_ref.dtype)


def torus_sum(values, axis, number, name):
    count, rows, width = values.shape
    side = 4
    half = rows // 2
    return pl.pallas_call(
        functools.partial(torus_sum_kernel, axis, side),
        out_shape=jax.ShapeDtypeStruct((rows, width), values.dtype),
        in_specs=[vmem()],
        out_specs=vmem(),
        scratch_shapes=[
            pltpu.VMEM((2, side - 1, side, half, width), values.dtype),
            pltpu.VMEM((2, 2, side // 2, half, width), values.dtype),
            pltpu.VMEM((2, side, half, width), values.dtype),
            pltpu.VMEM((2, side - 1, half, width), values.dtype),
            pltpu.SemaphoreType.DMA((2, 9)),
            pltpu.SemaphoreType.DMA((2, 9)),
        ],
        compiler_params=pltpu.CompilerParams(
            collective_id=number, has_side_effects=True, vmem_limit_bytes=40 * 1024 * 1024
        ),
        name=name,
    )(values.reshape(side, count // side, rows, width))


def local(
    hidden_in,
    cache_pool,
    project_in,
    project_out,
    norm_first,
    norm_second,
    router,
    gate_up,
    expert_down,
    lengths,
    prompt_pages,
    own_pages,
    groups,
    move_target,
    routes,
):
    rows_count = lax.axis_size("dp")
    fsdp_count = lax.axis_size("fsdp")
    my_row = lax.axis_index("dp")
    my_column = lax.axis_index("fsdp")
    req_local, model_width = hidden_in.shape
    req_row = req_local * fsdp_count
    movers = move_target.shape[1]
    staying = req_row - movers
    pages, page_len = cache_pool.shape[:2]
    head_cols = cache_pool.shape[3]
    expert_count = router.shape[1]
    rows_per_expert = rows_count // expert_count
    slots_row = (CAP + rows_per_expert - 1) // rows_per_expert
    units_here = gate_up.shape[3]
    features_here = gate_up.shape[1]

    same_core = [list(range(k, rows_count, rows_per_expert)) for k in range(rows_per_expert)]

    def spread_weights(values):
        return lax.all_to_all(
            values, "dp", split_axis=0, concat_axis=0, tiled=True, axis_index_groups=same_core
        )

    row_tokens = exchange(hidden_in, "fsdp", 0, "row_tokens", gather=True)
    row_tokens = row_tokens.reshape(req_row, model_width)
    weights = jnp.concatenate(
        [jnp.transpose(project_in, (1, 0, 2)), project_out.T[None]], axis=0
    )
    weights = lax.all_gather(weights, "dp", axis=1, tiled=True)
    weight_in, weight_out = weights[:3], weights[3]
    gate_cols, up_cols = gate_up[:, :, 0], gate_up[:, :, 1]
    row_tokens, gate_cols, up_cols = lax.optimization_barrier((row_tokens, gate_cols, up_cols))
    expert_down, weights = lax.optimization_barrier((expert_down, weights))
    swap = [(d, d ^ 1) for d in range(rows_count)]
    down_own = spread_weights(expert_down)

    group_hit = (
        groups[:, None] == jnp.arange(prompt_pages.shape[0], dtype=jnp.int32)[None, :]
    ).astype(jnp.int32)
    prompt_list = jnp.sum(group_hit[:, :, None] * prompt_pages[None, :, :], axis=1)
    page_list = jnp.concatenate([prompt_list, own_pages], axis=1)
    position = lax.dynamic_slice_in_dim(lengths, my_row * req_row, req_row)
    page_numbers = jnp.arange(pages, dtype=jnp.int32)
    limit = jnp.zeros((req_row, pages), jnp.int32)
    for j in range(page_list.shape[1]):
        valid = jnp.clip(position - page_len * j, 0, page_len)
        limit += jnp.where(page_list[:, j : j + 1] == page_numbers[None, :], valid[:, None], 0)

    heads_out = attention(row_tokens, norm_first, weight_in, position, limit, cache_pool)

    row_numbers = jnp.arange(rows_count, dtype=jnp.int32)
    send_select = (move_target[my_row][None, :] == row_numbers[:, None]).astype(BF16)
    leaving = jnp.concatenate([heads_out[staying:], row_tokens[staying:]], axis=1)
    leaving_send = jnp.dot(send_select, leaving, preferred_element_type=F32).astype(BF16)
    leaving_send, down_own = lax.optimization_barrier((leaving_send, down_own))
    down_own = down_own.reshape(-1, units_here)
    leaving_recv = exchange(leaving_send[:, None, :], "dp", 1, "leaving")[:, 0]
    leaving_recv, gate_cols = lax.optimization_barrier((leaving_recv, gate_cols))
    down_other = lax.ppermute(down_own, "dp", swap)
    gate_own = spread_weights(gate_cols)
    arrive_select = (move_target == my_row).astype(BF16)
    arrived = lax.dot_general(
        arrive_select, leaving_recv, (((0,), (0,)), ((), ())), preferred_element_type=F32
    ).astype(BF16)
    heads_row = jnp.concatenate([heads_out[:staying], arrived[:, :head_cols]], axis=0)
    mine_tokens = jnp.where(
        my_column == fsdp_count - 1, arrived[:, head_cols:], hidden_in
    )
    partial_out = dot_t(heads_row, weight_out).astype(BF16)
    attn_proj = exchange(
        partial_out.reshape(fsdp_count, req_local, model_width),
        "fsdp",
        2,
        "partial_out",
        reduce=F32,
    )
    resid = mine_tokens.astype(F32) + attn_proj
    moe_in = rms_scale(resid, norm_second).astype(BF16)
    moe_in, gate_own = lax.optimization_barrier((moe_in, gate_own))
    logits = jnp.dot(moe_in, router, preferred_element_type=F32)
    expert_ids = jnp.arange(expert_count, dtype=jnp.int32)
    picked = routes[:, :, None] == expert_ids[None, None, :]
    chosen = jnp.sum(jnp.where(picked, logits[:, None, :], 0.0), axis=-1)
    weight_pair = jnp.stack(
        [jax.nn.sigmoid(chosen[:, 0] - chosen[:, 1]), jax.nn.sigmoid(chosen[:, 1] - chosen[:, 0])],
        axis=1,
    )
    mix_expert = jnp.sum(picked.astype(F32) * weight_pair[:, :, None], axis=1)
    member = jnp.sum(picked.astype(jnp.int32), axis=1)
    rank_expert = jnp.cumsum(member, axis=0) - member
    expert_of_row = (row_numbers[:, None] // rows_per_expert == expert_ids[None, :]).astype(
        jnp.int32
    )
    replica_of_row = row_numbers % rows_per_expert
    member_row = jnp.sum(member[:, None, :] * expert_of_row[None, :, :], axis=-1)
    rank_row = jnp.sum(rank_expert[:, None, :] * expert_of_row[None, :, :], axis=-1)
    mix_row = jnp.sum(mix_expert[:, None, :] * expert_of_row[None, :, :].astype(F32), axis=-1)
    slot_ids = jnp.arange(slots_row, dtype=jnp.int32)
    wanted_rank = slot_ids[None, :, None] * rows_per_expert + replica_of_row[:, None, None]
    select = (member_row.T[:, None, :] == 1) & (rank_row.T[:, None, :] == wanted_rank)
    dispatch = jnp.einsum(
        "dst,tm->dsm", select.astype(BF16), moe_in, preferred_element_type=F32
    ).astype(BF16)
    by_core = dispatch.reshape(rows_count // 2, 2, slots_row, rows_count // 2, 2, features_here)
    half = model_width // 2
    cores = [by_core[:, :, :, :, c].reshape(rows_count // 2, 2, slots_row, half) for c in range(2)]
    dispatch = jnp.stack(
        [
            jnp.concatenate([cores[0][:, 0], cores[1][:, 0]], axis=-1),
            jnp.concatenate([cores[1][:, 1], cores[0][:, 1]], axis=-1),
        ],
        axis=1,
    ).reshape(rows_count, slots_row, model_width)
    gate_own = gate_own.reshape(-1, units_here)
    received = exchange(dispatch, "dp", 3, "dispatch")
    received, up_cols = lax.optimization_barrier((received, up_cols))
    gate_other = lax.ppermute(gate_own, "dp", swap)
    up_own = spread_weights(up_cols).reshape(-1, units_here)
    up_other = lax.ppermute(up_own, "dp", swap)
    expert_tokens = torus_gather(
        received.reshape(rows_count * slots_row, model_width), "fsdp", 4, "expert_tokens"
    )
    flattened = expert_tokens.reshape(-1, model_width)
    gate_part = jnp.dot(flattened[:, :half], gate_own, preferred_element_type=F32) + jnp.dot(
        flattened[:, half:], gate_other, preferred_element_type=F32
    )
    up_part = jnp.dot(flattened[:, :half], up_own, preferred_element_type=F32) + jnp.dot(
        flattened[:, half:], up_other, preferred_element_type=F32
    )
    activation = (jax.nn.silu(gate_part) * up_part).astype(BF16)
    expert_y = jnp.concatenate(
        [dot_t(activation, down_own).astype(BF16), dot_t(activation, down_other).astype(BF16)],
        axis=1,
    )
    returned = torus_sum(
        expert_y.reshape(fsdp_count, rows_count * slots_row, model_width),
        "fsdp",
        5,
        "expert_sums",
    )
    back_rows = exchange(
        returned.reshape(rows_count, slots_row, model_width), "dp", 6, "back_rows"
    )
    coefficient = select.astype(F32) * mix_row.T[:, None, :]
    coefficient = coefficient.reshape(rows_count // 2, 2, slots_row, req_local)
    back_rows = back_rows.astype(F32).reshape(rows_count // 2, 2, slots_row, model_width)
    sums = [
        jnp.einsum(
            "dst,dsm->tm", coefficient[:, c], back_rows[:, c], precision=lax.Precision.HIGHEST
        )
        for c in range(2)
    ]
    by_core = [
        sums[0][:, :half] + sums[1][:, half:],
        sums[0][:, half:] + sums[1][:, :half],
    ]
    moe_total = jnp.stack(
        [part.reshape(req_local, rows_count // 2, features_here) for part in by_core], axis=2
    ).reshape(req_local, model_width)
    return (resid + moe_total).astype(BF16)


def solution(mesh):
    placed = (
        P(("dp", "fsdp"), None),
        P("dp", None, None, "fsdp"),
        P("dp", None, "fsdp"),
        P("fsdp", "dp"),
        P(),
        P(),
        P(),
        P(None, "dp", None, "fsdp"),
        P(None, "dp", "fsdp"),
        P(),
        P("dp", None),
        P("dp", None),
        P("dp"),
        P(),
        P(("dp", "fsdp"), None),
    )
    return jax.shard_map(
        local, mesh=mesh, in_specs=placed, out_specs=P(("dp", "fsdp"), None), check_vma=False
    )
```

```python
import functools

import jax
import jax.numpy as jnp
from jax import lax
from jax.experimental import pallas as pl
from jax.experimental.pallas import tpu as pltpu
from jax.sharding import PartitionSpec as P

HD = 64
CAP = 4
LOW = -1e30
F32 = jnp.float32
BF16 = jnp.bfloat16


def vmem():
    return pl.BlockSpec(memory_space=pltpu.VMEM)


def rms_scale(values, scaling):
    return (
        values
        * lax.rsqrt(jnp.mean(values * values, axis=-1, keepdims=True) + 1e-06)
        * scaling.astype(F32)
    )


def dot_t(left, right):
    return lax.dot_general(left, right, (((1,), (1,)), ((), ())), preferred_element_type=F32)


def attention_kernel(
    page_len, tokens_ref, norm_ref, weight_ref, cos_ref, sin_ref, limit_ref, cache_ref, out_ref, wide_ref, score_ref
):
    pages = limit_ref.shape[1]
    count, width = out_ref.shape
    heads = width // HD
    wide_ref[...] = cache_ref[...].astype(F32)
    normed = rms_scale(tokens_ref[...].astype(F32), norm_ref[...]).astype(BF16)
    parts = [jnp.dot(normed, weight_ref[i], preferred_element_type=F32) for i in range(3)]
    lane = lax.broadcasted_iota(jnp.int32, (count, width), 1)
    low_half = lane % HD < HD // 2

    def rotate(values):
        partner = jnp.where(
            low_half,
            pltpu.roll(values, width - HD // 2, 1),
            pltpu.roll(values, HD // 2, 1),
        )
        return (values * cos_ref[...] + partner * sin_ref[...]).astype(BF16)

    query = rotate(parts[0])
    key_new = rotate(parts[1])
    value_new = parts[2].astype(BF16)
    head_lane = lax.broadcasted_iota(jnp.int32, (heads, count, width), 2) // HD
    head_row = lax.broadcasted_iota(jnp.int32, (heads, count, width), 0)
    wide_query = query.astype(F32)
    spread = jnp.where(head_lane == head_row, wide_query[None], 0.0)
    scale = HD ** (-0.5)
    own_score = jnp.sum(spread * key_new.astype(F32)[None], axis=-1, keepdims=True) * scale
    spread_query = spread.reshape(heads * count, width).astype(BF16)
    own_score = own_score.reshape(heads * count, 1)

    def score_step(u, highest):
        keys = wide_ref[pl.ds(2 * u, pages, stride=2 * page_len), :].astype(BF16)
        scores = dot_t(spread_query, keys) * scale
        scores = jnp.where((limit_ref[...] > u)[None], scores.reshape(heads, count, pages), LOW)
        scores = scores.reshape(heads * count, pages)
        score_ref[u] = scores
        return jnp.maximum(highest, scores)

    highest = lax.fori_loop(
        0, page_len, score_step, jnp.full((heads * count, pages), LOW, F32)
    )
    highest = jnp.maximum(jnp.max(highest, axis=-1, keepdims=True), own_score)

    def value_step(u, carry):
        total, mixture = carry
        weights = jnp.exp(score_ref[u] - highest)
        values = wide_ref[pl.ds(2 * u + 1, pages, stride=2 * page_len), :].astype(BF16)
        mixture = mixture + jnp.dot(weights.astype(BF16), values, preferred_element_type=F32)
        return total + jnp.sum(weights, axis=-1, keepdims=True), mixture

    weight_own = jnp.exp(own_score - highest)
    total, mixture = lax.fori_loop(
        0,
        page_len,
        value_step,
        (weight_own, jnp.zeros((heads * count, width), F32)),
    )
    mixture = (mixture / total).reshape(heads, count, width)
    prob_own = (weight_own / total).astype(BF16).astype(F32).reshape(heads, count, 1)
    mixture = mixture + prob_own * value_new.astype(F32)[None]
    out_ref[...] = jnp.sum(jnp.where(head_lane == head_row, mixture, 0.0), axis=0).astype(BF16)


def attention(tokens, norm, weight, position, limit, cache_pool):
    count = tokens.shape[0]
    pages, page_len, _, width = cache_pool.shape
    channel = (jnp.arange(width, dtype=jnp.int32) % (HD // 2)).astype(F32)
    inverse = jnp.exp(-jnp.log(10000.0) * 2.0 * channel / HD)
    angles = position.astype(F32)[:, None] * inverse
    sign = jnp.where(jnp.arange(width) % HD < HD // 2, -1.0, 1.0)
    rows = pages * page_len * 2
    return pl.pallas_call(
        functools.partial(attention_kernel, page_len),
        out_shape=jax.ShapeDtypeStruct((count, width), BF16),
        in_specs=[vmem()] * 7,
        out_specs=vmem(),
        scratch_shapes=[
            pltpu.VMEM((rows, width), F32),
            pltpu.VMEM((page_len, count * (width // HD), pages), F32),
        ],
        compiler_params=pltpu.CompilerParams(vmem_limit_bytes=56 * 1024 * 1024),
        cost_estimate=pl.CostEstimate(
            flops=4 * count * width * rows, bytes_accessed=60_000_000, transcendentals=0
        ),
        name="attention",
    )(
        tokens,
        norm[None, :],
        weight,
        jnp.cos(angles),
        jnp.sin(angles) * sign,
        limit,
        cache_pool.reshape(rows, width),
    )


def exchange_kernel(axis, count, gather, reduce, src_ref, out_ref, *scratch):
    land_ref = scratch[0] if reduce else out_ref
    send_sem, recv_sem, own_sem = scratch[-3:]
    me = lax.axis_index(axis)
    barrier = pltpu.get_barrier_semaphore()
    for step in range(1, count):
        pl.semaphore_signal(
            barrier,
            inc=1,
            device_id={axis: lax.rem(me + step, count)},
            device_id_type=pl.DeviceIdType.MESH,
        )
    pl.semaphore_wait(barrier, count - 1)
    copies = []
    for step in range(1, count):
        peer = lax.rem(me + step, count)
        copy = pltpu.make_async_remote_copy(
            src_ref=src_ref if gather else src_ref.at[peer],
            dst_ref=land_ref.at[me],
            send_sem=send_sem.at[step],
            recv_sem=recv_sem.at[step],
            device_id={axis: peer},
            device_id_type=pl.DeviceIdType.MESH,
        )
        copy.start()
        copies.append(copy)
    own = pltpu.make_async_copy(src_ref if gather else src_ref.at[me], land_ref.at[me], own_sem)
    own.start()
    own.wait()
    for copy in copies:
        copy.wait()
    if reduce:
        width = land_ref.shape[2]
        block = width // 6
        for start in range(0, width, block):
            total = land_ref[0, :, start : start + block].astype(F32)
            for source in range(1, count):
                total = total + land_ref[source, :, start : start + block].astype(F32)
            out_ref[:, start : start + block] = total.astype(out_ref.dtype)


def exchange(values, axis, number, name, gather=False, reduce=None):
    count = lax.axis_size(axis)
    block = values.shape if gather else values.shape[1:]
    landing = (count,) + block
    semaphores = [
        pltpu.SemaphoreType.DMA((count,)),
        pltpu.SemaphoreType.DMA((count,)),
        pltpu.SemaphoreType.DMA,
    ]
    if reduce is None:
        result = jax.ShapeDtypeStruct(landing, values.dtype)
        scratch = semaphores
    else:
        result = jax.ShapeDtypeStruct(block, reduce)
        scratch = [pltpu.VMEM(landing, values.dtype)] + semaphores
    return pl.pallas_call(
        functools.partial(exchange_kernel, axis, count, gather, reduce is not None),
        out_shape=result,
        in_specs=[vmem()],
        out_specs=vmem(),
        scratch_shapes=scratch,
        compiler_params=pltpu.CompilerParams(collective_id=number, has_side_effects=True),
        cost_estimate=pl.CostEstimate(flops=0, bytes_accessed=200_000_000, transcendentals=0),
        name=name,
    )(values)


def prologue_kernel(
    ring, count, token_ref, weight_ref, tokens_out, weights_out,
    token_send, token_recv, right_send, right_recv, left_send, left_recv,
    pair_send, pair_recv, own_sem,
):
    me = lax.axis_index("fsdp")
    row = lax.axis_index("dp")
    chip, core = row // 2, lax.rem(row, 2)

    def place(step):
        return lax.rem(chip + step, ring) * 2 + core

    partner = {"dp": chip * 2 + (1 - core)}
    after = {"dp": place(1)}
    before = {"dp": place(ring - 1)}
    peers = [{"fsdp": lax.rem(me + step, count)} for step in range(1, count)]
    barrier = pltpu.get_barrier_semaphore()
    for device in peers + [partner, after, before]:
        pl.semaphore_signal(
            barrier, inc=1, device_id=device, device_id_type=pl.DeviceIdType.MESH
        )
    pl.semaphore_wait(barrier, count + 2)

    def send(src, dst, send_sem, recv_sem, device):
        copy = pltpu.make_async_remote_copy(
            src_ref=src,
            dst_ref=dst,
            send_sem=send_sem,
            recv_sem=recv_sem,
            device_id=device,
            device_id_type=pl.DeviceIdType.MESH,
        )
        copy.start()
        return copy

    def slot(step):
        return weights_out.at[:, place(step)]

    rights = ring // 2
    lefts = ring - 1 - rights
    right = send(weight_ref, slot(0), right_send.at[0], right_recv.at[0], after)
    left = send(weight_ref, slot(0), left_send.at[0], left_recv.at[0], before)
    tail = [send(weight_ref, slot(0), pair_send.at[0], pair_recv.at[0], partner)]
    for step, device in enumerate(peers):
        tail.append(
            send(token_ref, tokens_out.at[me], token_send.at[step], token_recv.at[step], device)
        )
    own = [
        pltpu.make_async_copy(weight_ref, slot(0), own_sem.at[0]),
        pltpu.make_async_copy(token_ref, tokens_out.at[me], own_sem.at[1]),
    ]
    for copy in own:
        copy.start()
    for s in range(1, rights + 1):
        right.wait()
        block = slot(ring - s)
        if s < rights:
            right = send(block, block, right_send.at[s], right_recv.at[s], after)
        tail.append(send(block, block, pair_send.at[s], pair_recv.at[s], partner))
        if s <= lefts:
            left.wait()
            block = slot(s)
            if s < lefts:
                left = send(block, block, left_send.at[s], left_recv.at[s], before)
            tail.append(
                send(block, block, pair_send.at[rights + s], pair_recv.at[rights + s], partner)
            )
    for copy in own + tail:
        copy.wait()


def prologue(tokens, weights, number):
    rows_count = lax.axis_size("dp")
    count = lax.axis_size("fsdp")
    ring = rows_count // 2
    parts, depth, width = weights.shape
    return pl.pallas_call(
        functools.partial(prologue_kernel, ring, count),
        out_shape=(
            jax.ShapeDtypeStruct((count,) + tokens.shape, tokens.dtype),
            jax.ShapeDtypeStruct((parts, rows_count, depth, width), weights.dtype),
        ),
        in_specs=[vmem()] * 2,
        out_specs=(vmem(), vmem()),
        scratch_shapes=[
            pltpu.SemaphoreType.DMA((count - 1,)),
            pltpu.SemaphoreType.DMA((count - 1,)),
            pltpu.SemaphoreType.DMA((ring,)),
            pltpu.SemaphoreType.DMA((ring,)),
            pltpu.SemaphoreType.DMA((ring,)),
            pltpu.SemaphoreType.DMA((ring,)),
            pltpu.SemaphoreType.DMA((ring,)),
            pltpu.SemaphoreType.DMA((ring,)),
            pltpu.SemaphoreType.DMA((2,)),
        ],
        compiler_params=pltpu.CompilerParams(collective_id=number, has_side_effects=True),
        name="prologue",
    )(tokens, weights)


def torus_ids(axis, side):
    me = lax.axis_index(axis)
    y, x = me // side, lax.rem(me, side)

    def peer(along_y, step):
        if along_y:
            return {axis: lax.rem(y + step, side) * side + x}
        return {axis: y * side + lax.rem(x + step, side)}

    return y, x, peer


def torus_barrier(peer, side):
    barrier = pltpu.get_barrier_semaphore()
    for along_y in (False, True):
        for step in range(1, side):
            pl.semaphore_signal(
                barrier,
                inc=1,
                device_id=peer(along_y, step),
                device_id_type=pl.DeviceIdType.MESH,
            )
    pl.semaphore_wait(barrier, 2 * (side - 1))


def torus_gather_kernel(axis, side, src_ref, out_ref, send_sem, recv_sem, own_sem):
    y, x, peer = torus_ids(axis, side)
    half = src_ref.shape[0] // 2
    rows = [pl.ds(0, half), pl.ds(half, half)]
    part = [pl.ds(0, side // 2), pl.ds(side // 2, side - side // 2)]
    torus_barrier(peer, side)

    def send(h, number, src, dst, device):
        copy = pltpu.make_async_remote_copy(
            src_ref=src,
            dst_ref=dst,
            send_sem=send_sem.at[h, number],
            recv_sem=recv_sem.at[h, number],
            device_id=device,
            device_id_type=pl.DeviceIdType.MESH,
        )
        copy.start()
        return copy

    first = [
        [
            send(h, step - 1, src_ref.at[rows[h]], out_ref.at[y, x, rows[h]], peer(h == 1, step))
            for step in range(1, side)
        ]
        for h in range(2)
    ]
    own = pltpu.make_async_copy(src_ref, out_ref.at[y, x], own_sem)
    own.start()
    own.wait()

    def group(h, step, blocks):
        if h == 0:
            return out_ref.at[lax.rem(y + step, side), blocks, rows[h]]
        return out_ref.at[blocks, lax.rem(x + step, side), rows[h]]

    whole = pl.ds(0, side)
    second = []
    for h in range(2):
        for copy in first[h]:
            copy.wait()
        second.append(
            [
                send(h, 3, group(h, 0, whole), group(h, 0, whole), peer(h == 0, 1)),
                send(h, 4, group(h, 0, whole), group(h, 0, whole), peer(h == 0, side - 1)),
            ]
        )
    third = []
    for h in range(2):
        for k, back in ((0, side - 1), (1, 1)):
            second[h][k].wait()
            source = group(h, back, part[k])
            third.append(send(h, 5 + k, source, source, peer(h == 0, side - back)))
    for copy in third:
        copy.wait()


def torus_gather(values, axis, number, name):
    count = lax.axis_size(axis)
    side = 4
    return pl.pallas_call(
        functools.partial(torus_gather_kernel, axis, side),
        out_shape=jax.ShapeDtypeStruct((side, count // side) + values.shape, values.dtype),
        in_specs=[vmem()],
        out_specs=vmem(),
        scratch_shapes=[
            pltpu.SemaphoreType.DMA((2, 7)),
            pltpu.SemaphoreType.DMA((2, 7)),
            pltpu.SemaphoreType.DMA,
        ],
        compiler_params=pltpu.CompilerParams(collective_id=number, has_side_effects=True),
        cost_estimate=pl.CostEstimate(flops=0, bytes_accessed=60_000_000, transcendentals=0),
        name=name,
    )(values)


def torus_sum_kernel(
    axis, side, src_ref, out_ref, land_ref, relay_ref, sum_ref, last_ref, send_sem, recv_sem
):
    y, x, peer = torus_ids(axis, side)
    half = src_ref.shape[2] // 2
    width = src_ref.shape[3]
    block = width // 3
    rows = [pl.ds(0, half), pl.ds(half, half)]
    part = [pl.ds(0, side // 2), pl.ds(side // 2, side - side // 2)]
    whole = pl.ds(0, side)
    torus_barrier(peer, side)

    def send(h, number, src, dst, device):
        copy = pltpu.make_async_remote_copy(
            src_ref=src,
            dst_ref=dst,
            send_sem=send_sem.at[h, number],
            recv_sem=recv_sem.at[h, number],
            device_id=device,
            device_id_type=pl.DeviceIdType.MESH,
        )
        copy.start()
        return copy

    def terms(h, step, blocks):
        if h == 0:
            return src_ref.at[blocks, lax.rem(x + step, side), rows[h]]
        return src_ref.at[lax.rem(y + step, side), blocks, rows[h]]

    far, near, relays = [], [], []
    for h in range(2):
        far.append(
            [
                send(h, 0, terms(h, 2, part[0]), relay_ref.at[h, 0], peer(h == 1, 1)),
                send(h, 1, terms(h, 2, part[1]), relay_ref.at[h, 1], peer(h == 1, side - 1)),
            ]
        )
    for h in range(2):
        near.append(
            [
                send(h, 2, terms(h, 1, whole), land_ref.at[h, 0], peer(h == 1, 1)),
                send(h, 3, terms(h, side - 1, whole), land_ref.at[h, 2], peer(h == 1, side - 1)),
            ]
        )
    for h in range(2):
        for k, step in ((0, 1), (1, side - 1)):
            far[h][k].wait()
            relays.append(
                send(
                    h, 4 + k, relay_ref.at[h, k], land_ref.at[h, 1, part[k]], peer(h == 1, step)
                )
            )
    for h in range(2):
        for copy in near[h]:
            copy.wait()
    for copy in relays:
        copy.wait()
    last = []
    for h in range(2):
        for b in range(side):
            for start in range(0, width, block):
                cols = slice(start, start + block)
                if h == 0:
                    total = src_ref[b, x, 0:half, cols].astype(F32)
                else:
                    total = src_ref[y, b, half : 2 * half, cols].astype(F32)
                for k in range(side - 1):
                    total = total + land_ref[h, k, b, :, cols].astype(F32)
                sum_ref[h, b, :, cols] = total.astype(sum_ref.dtype)
        mine = y if h == 0 else x
        for step in range(1, side):
            last.append(
                send(
                    h,
                    5 + step,
                    sum_ref.at[h, lax.rem(mine + step, side)],
                    last_ref.at[h, step - 1],
                    peer(h == 0, step),
                )
            )
    for copy in last:
        copy.wait()
    for h in range(2):
        mine = y if h == 0 else x
        for start in range(0, width, block):
            cols = slice(start, start + block)
            total = sum_ref[h, mine, :, cols].astype(F32)
            for k in range(side - 1):
                total = total + last_ref[h, k, :, cols].astype(F32)
            out_ref[h * half : (h + 1) * half, cols] = total.astype(out_ref.dtype)


def torus_sum(values, axis, number, name):
    count, rows, width = values.shape
    side = 4
    half = rows // 2
    return pl.pallas_call(
        functools.partial(torus_sum_kernel, axis, side),
        out_shape=jax.ShapeDtypeStruct((rows, width), values.dtype),
        in_specs=[vmem()],
        out_specs=vmem(),
        scratch_shapes=[
            pltpu.VMEM((2, side - 1, side, half, width), values.dtype),
            pltpu.VMEM((2, 2, side // 2, half, width), values.dtype),
            pltpu.VMEM((2, side, half, width), values.dtype),
            pltpu.VMEM((2, side - 1, half, width), values.dtype),
            pltpu.SemaphoreType.DMA((2, 9)),
            pltpu.SemaphoreType.DMA((2, 9)),
        ],
        compiler_params=pltpu.CompilerParams(
            collective_id=number, has_side_effects=True, vmem_limit_bytes=40 * 1024 * 1024
        ),
        name=name,
    )(values.reshape(side, count // side, rows, width))


def local(
    hidden_in,
    cache_pool,
    project_in,
    project_out,
    norm_first,
    norm_second,
    router,
    gate_up,
    expert_down,
    lengths,
    prompt_pages,
    own_pages,
    groups,
    move_target,
    routes,
):
    rows_count = lax.axis_size("dp")
    fsdp_count = lax.axis_size("fsdp")
    my_row = lax.axis_index("dp")
    my_column = lax.axis_index("fsdp")
    req_local, model_width = hidden_in.shape
    req_row = req_local * fsdp_count
    movers = move_target.shape[1]
    staying = req_row - movers
    pages, page_len = cache_pool.shape[:2]
    head_cols = cache_pool.shape[3]
    expert_count = router.shape[1]
    rows_per_expert = rows_count // expert_count
    slots_row = (CAP + rows_per_expert - 1) // rows_per_expert
    units_here = gate_up.shape[3]
    features_here = gate_up.shape[1]

    same_core = [list(range(k, rows_count, rows_per_expert)) for k in range(rows_per_expert)]

    def spread_weights(values):
        return lax.all_to_all(
            values, "dp", split_axis=0, concat_axis=0, tiled=True, axis_index_groups=same_core
        )

    weights = jnp.concatenate(
        [jnp.transpose(project_in, (1, 0, 2)), project_out.T[None]], axis=0
    )
    row_tokens, weights = prologue(hidden_in, weights, 0)
    row_tokens = row_tokens.reshape(req_row, model_width)
    weights = weights.reshape(weights.shape[0], model_width, head_cols)
    weight_out = weights[3]
    gate_cols = gate_up[:, :, 0]
    expert_down, weights, gate_cols = lax.optimization_barrier((expert_down, weights, gate_cols))
    swap = [(d, d ^ 1) for d in range(rows_count)]
    down_own = spread_weights(expert_down)

    group_hit = (
        groups[:, None] == jnp.arange(prompt_pages.shape[0], dtype=jnp.int32)[None, :]
    ).astype(jnp.int32)
    prompt_list = jnp.sum(group_hit[:, :, None] * prompt_pages[None, :, :], axis=1)
    page_list = jnp.concatenate([prompt_list, own_pages], axis=1)
    position = lax.dynamic_slice_in_dim(lengths, my_row * req_row, req_row)
    page_numbers = jnp.arange(pages, dtype=jnp.int32)
    limit = jnp.zeros((req_row, pages), jnp.int32)
    for j in range(page_list.shape[1]):
        valid = jnp.clip(position - page_len * j, 0, page_len)
        limit += jnp.where(page_list[:, j : j + 1] == page_numbers[None, :], valid[:, None], 0)

    heads_out = attention(row_tokens, norm_first, weights, position, limit, cache_pool)

    row_numbers = jnp.arange(rows_count, dtype=jnp.int32)
    send_select = (move_target[my_row][None, :] == row_numbers[:, None]).astype(BF16)
    leaving = jnp.concatenate([heads_out[staying:], row_tokens[staying:]], axis=1)
    leaving_send = jnp.dot(send_select, leaving, preferred_element_type=F32).astype(BF16)
    leaving_send, down_own = lax.optimization_barrier((leaving_send, down_own))
    down_own = down_own.reshape(-1, units_here)
    leaving_recv = exchange(leaving_send[:, None, :], "dp", 1, "leaving")[:, 0]
    leaving_recv, gate_cols = lax.optimization_barrier((leaving_recv, gate_cols))
    down_other = lax.ppermute(down_own, "dp", swap)
    gate_own = spread_weights(gate_cols)
    arrive_select = (move_target == my_row).astype(BF16)
    arrived = lax.dot_general(
        arrive_select, leaving_recv, (((0,), (0,)), ((), ())), preferred_element_type=F32
    ).astype(BF16)
    heads_row = jnp.concatenate([heads_out[:staying], arrived[:, :head_cols]], axis=0)
    mine_tokens = jnp.where(
        my_column == fsdp_count - 1, arrived[:, head_cols:], hidden_in
    )
    partial_out = dot_t(heads_row, weight_out).astype(BF16)
    attn_proj = exchange(
        partial_out.reshape(fsdp_count, req_local, model_width),
        "fsdp",
        2,
        "partial_out",
        reduce=F32,
    )
    attn_proj, gate_up = lax.optimization_barrier((attn_proj, gate_up))
    up_cols = gate_up[:, :, 1]
    resid = mine_tokens.astype(F32) + attn_proj
    moe_in = rms_scale(resid, norm_second).astype(BF16)
    moe_in, gate_own, up_cols = lax.optimization_barrier((moe_in, gate_own, up_cols))
    logits = jnp.dot(moe_in, router, preferred_element_type=F32)
    expert_ids = jnp.arange(expert_count, dtype=jnp.int32)
    picked = routes[:, :, None] == expert_ids[None, None, :]
    chosen = jnp.sum(jnp.where(picked, logits[:, None, :], 0.0), axis=-1)
    weight_pair = jnp.stack(
        [jax.nn.sigmoid(chosen[:, 0] - chosen[:, 1]), jax.nn.sigmoid(chosen[:, 1] - chosen[:, 0])],
        axis=1,
    )
    mix_expert = jnp.sum(picked.astype(F32) * weight_pair[:, :, None], axis=1)
    member = jnp.sum(picked.astype(jnp.int32), axis=1)
    rank_expert = jnp.cumsum(member, axis=0) - member
    expert_of_row = (row_numbers[:, None] // rows_per_expert == expert_ids[None, :]).astype(
        jnp.int32
    )
    replica_of_row = row_numbers % rows_per_expert
    member_row = jnp.sum(member[:, None, :] * expert_of_row[None, :, :], axis=-1)
    rank_row = jnp.sum(rank_expert[:, None, :] * expert_of_row[None, :, :], axis=-1)
    mix_row = jnp.sum(mix_expert[:, None, :] * expert_of_row[None, :, :].astype(F32), axis=-1)
    slot_ids = jnp.arange(slots_row, dtype=jnp.int32)
    wanted_rank = slot_ids[None, :, None] * rows_per_expert + replica_of_row[:, None, None]
    select = (member_row.T[:, None, :] == 1) & (rank_row.T[:, None, :] == wanted_rank)
    dispatch = jnp.einsum(
        "dst,tm->dsm", select.astype(BF16), moe_in, preferred_element_type=F32
    ).astype(BF16)
    by_core = dispatch.reshape(rows_count // 2, 2, slots_row, rows_count // 2, 2, features_here)
    half = model_width // 2
    cores = [by_core[:, :, :, :, c].reshape(rows_count // 2, 2, slots_row, half) for c in range(2)]
    dispatch = jnp.stack(
        [
            jnp.concatenate([cores[0][:, 0], cores[1][:, 0]], axis=-1),
            jnp.concatenate([cores[1][:, 1], cores[0][:, 1]], axis=-1),
        ],
        axis=1,
    ).reshape(rows_count, slots_row, model_width)
    gate_own = gate_own.reshape(-1, units_here)
    received = exchange(dispatch, "dp", 3, "dispatch")
    received, up_cols = lax.optimization_barrier((received, up_cols))
    gate_other = lax.ppermute(gate_own, "dp", swap)
    up_own = spread_weights(up_cols).reshape(-1, units_here)
    up_other = lax.ppermute(up_own, "dp", swap)
    expert_tokens = torus_gather(
        received.reshape(rows_count * slots_row, model_width), "fsdp", 4, "expert_tokens"
    )
    flattened = expert_tokens.reshape(-1, model_width)
    gate_part = jnp.dot(flattened[:, :half], gate_own, preferred_element_type=F32) + jnp.dot(
        flattened[:, half:], gate_other, preferred_element_type=F32
    )
    up_part = jnp.dot(flattened[:, :half], up_own, preferred_element_type=F32) + jnp.dot(
        flattened[:, half:], up_other, preferred_element_type=F32
    )
    activation = (jax.nn.silu(gate_part) * up_part).astype(BF16)
    expert_y = jnp.concatenate(
        [dot_t(activation, down_own).astype(BF16), dot_t(activation, down_other).astype(BF16)],
        axis=1,
    )
    returned = torus_sum(
        expert_y.reshape(fsdp_count, rows_count * slots_row, model_width),
        "fsdp",
        5,
        "expert_sums",
    )
    back_rows = exchange(
        returned.reshape(rows_count, slots_row, model_width), "dp", 6, "back_rows"
    )
    coefficient = select.astype(F32) * mix_row.T[:, None, :]
    coefficient = coefficient.reshape(rows_count // 2, 2, slots_row, req_local)
    back_rows = back_rows.astype(F32).reshape(rows_count // 2, 2, slots_row, model_width)
    sums = [
        jnp.einsum(
            "dst,dsm->tm", coefficient[:, c], back_rows[:, c], precision=lax.Precision.HIGHEST
        )
        for c in range(2)
    ]
    by_core = [
        sums[0][:, :half] + sums[1][:, half:],
        sums[0][:, half:] + sums[1][:, :half],
    ]
    moe_total = jnp.stack(
        [part.reshape(req_local, rows_count // 2, features_here) for part in by_core], axis=2
    ).reshape(req_local, model_width)
    return (resid + moe_total).astype(BF16)


def solution(mesh):
    placed = (
        P(("dp", "fsdp"), None),
        P("dp", None, None, "fsdp"),
        P("dp", None, "fsdp"),
        P("fsdp", "dp"),
        P(),
        P(),
        P(),
        P(None, "dp", None, "fsdp"),
        P(None, "dp", "fsdp"),
        P(),
        P("dp", None),
        P("dp", None),
        P("dp"),
        P(),
        P(("dp", "fsdp"), None),
    )
    return jax.shard_map(
        local, mesh=mesh, in_specs=placed, out_specs=P(("dp", "fsdp"), None), check_vma=False
    )
```

```python
import functools

import jax
import jax.numpy as jnp
from jax import lax
from jax.experimental import pallas as pl
from jax.experimental.pallas import tpu as pltpu
from jax.sharding import PartitionSpec as P

HD = 64
CAP = 4
LOW = -1e30
F32 = jnp.float32
BF16 = jnp.bfloat16


def vmem():
    return pl.BlockSpec(memory_space=pltpu.VMEM)


def rms_scale(values, scaling):
    return (
        values
        * lax.rsqrt(jnp.mean(values * values, axis=-1, keepdims=True) + 1e-06)
        * scaling.astype(F32)
    )


def dot_t(left, right):
    return lax.dot_general(left, right, (((1,), (1,)), ((), ())), preferred_element_type=F32)


def attention_kernel(
    page_len, tokens_ref, norm_ref, weight_ref, cos_ref, sin_ref, limit_ref, cache_ref, out_ref, wide_ref, score_ref
):
    pages = limit_ref.shape[1]
    count, width = out_ref.shape
    heads = width // HD
    wide_ref[...] = cache_ref[...].astype(F32)
    normed = rms_scale(tokens_ref[...].astype(F32), norm_ref[...]).astype(BF16)
    parts = [jnp.dot(normed, weight_ref[i], preferred_element_type=F32) for i in range(3)]
    lane = lax.broadcasted_iota(jnp.int32, (count, width), 1)
    low_half = lane % HD < HD // 2

    def rotate(values):
        partner = jnp.where(
            low_half,
            pltpu.roll(values, width - HD // 2, 1),
            pltpu.roll(values, HD // 2, 1),
        )
        return (values * cos_ref[...] + partner * sin_ref[...]).astype(BF16)

    query = rotate(parts[0])
    key_new = rotate(parts[1])
    value_new = parts[2].astype(BF16)
    head_lane = lax.broadcasted_iota(jnp.int32, (heads, count, width), 2) // HD
    head_row = lax.broadcasted_iota(jnp.int32, (heads, count, width), 0)
    wide_query = query.astype(F32)
    spread = jnp.where(head_lane == head_row, wide_query[None], 0.0)
    scale = HD ** (-0.5)
    own_score = jnp.sum(spread * key_new.astype(F32)[None], axis=-1, keepdims=True) * scale
    spread_query = spread.reshape(heads * count, width).astype(BF16)
    own_score = own_score.reshape(heads * count, 1)

    def score_step(u, highest):
        keys = wide_ref[pl.ds(2 * u, pages, stride=2 * page_len), :].astype(BF16)
        scores = dot_t(spread_query, keys) * scale
        scores = jnp.where((limit_ref[...] > u)[None], scores.reshape(heads, count, pages), LOW)
        scores = scores.reshape(heads * count, pages)
        score_ref[u] = scores
        return jnp.maximum(highest, scores)

    highest = lax.fori_loop(
        0, page_len, score_step, jnp.full((heads * count, pages), LOW, F32)
    )
    highest = jnp.maximum(jnp.max(highest, axis=-1, keepdims=True), own_score)

    def value_step(u, carry):
        total, mixture = carry
        weights = jnp.exp(score_ref[u] - highest)
        values = wide_ref[pl.ds(2 * u + 1, pages, stride=2 * page_len), :].astype(BF16)
        mixture = mixture + jnp.dot(weights.astype(BF16), values, preferred_element_type=F32)
        return total + jnp.sum(weights, axis=-1, keepdims=True), mixture

    weight_own = jnp.exp(own_score - highest)
    total, mixture = lax.fori_loop(
        0,
        page_len,
        value_step,
        (weight_own, jnp.zeros((heads * count, width), F32)),
    )
    mixture = (mixture / total).reshape(heads, count, width)
    prob_own = (weight_own / total).astype(BF16).astype(F32).reshape(heads, count, 1)
    mixture = mixture + prob_own * value_new.astype(F32)[None]
    out_ref[...] = jnp.sum(jnp.where(head_lane == head_row, mixture, 0.0), axis=0).astype(BF16)


def attention(tokens, norm, weight, position, limit, cache_pool):
    count = tokens.shape[0]
    pages, page_len, _, width = cache_pool.shape
    channel = (jnp.arange(width, dtype=jnp.int32) % (HD // 2)).astype(F32)
    inverse = jnp.exp(-jnp.log(10000.0) * 2.0 * channel / HD)
    angles = position.astype(F32)[:, None] * inverse
    sign = jnp.where(jnp.arange(width) % HD < HD // 2, -1.0, 1.0)
    rows = pages * page_len * 2
    return pl.pallas_call(
        functools.partial(attention_kernel, page_len),
        out_shape=jax.ShapeDtypeStruct((count, width), BF16),
        in_specs=[vmem()] * 7,
        out_specs=vmem(),
        scratch_shapes=[
            pltpu.VMEM((rows, width), F32),
            pltpu.VMEM((page_len, count * (width // HD), pages), F32),
        ],
        compiler_params=pltpu.CompilerParams(vmem_limit_bytes=56 * 1024 * 1024),
        cost_estimate=pl.CostEstimate(
            flops=4 * count * width * rows, bytes_accessed=60_000_000, transcendentals=0
        ),
        name="attention",
    )(
        tokens,
        norm[None, :],
        weight,
        jnp.cos(angles),
        jnp.sin(angles) * sign,
        limit,
        cache_pool.reshape(rows, width),
    )


def exchange_kernel(axis, count, gather, reduce, src_ref, out_ref, *scratch):
    land_ref = scratch[0] if reduce else out_ref
    send_sem, recv_sem, own_sem = scratch[-3:]
    me = lax.axis_index(axis)
    barrier = pltpu.get_barrier_semaphore()
    for step in range(1, count):
        pl.semaphore_signal(
            barrier,
            inc=1,
            device_id={axis: lax.rem(me + step, count)},
            device_id_type=pl.DeviceIdType.MESH,
        )
    pl.semaphore_wait(barrier, count - 1)
    copies = []
    for step in range(1, count):
        peer = lax.rem(me + step, count)
        copy = pltpu.make_async_remote_copy(
            src_ref=src_ref if gather else src_ref.at[peer],
            dst_ref=land_ref.at[me],
            send_sem=send_sem.at[step],
            recv_sem=recv_sem.at[step],
            device_id={axis: peer},
            device_id_type=pl.DeviceIdType.MESH,
        )
        copy.start()
        copies.append(copy)
    own = pltpu.make_async_copy(src_ref if gather else src_ref.at[me], land_ref.at[me], own_sem)
    own.start()
    own.wait()
    for copy in copies:
        copy.wait()
    if reduce:
        width = land_ref.shape[2]
        block = width // 6
        for start in range(0, width, block):
            total = land_ref[0, :, start : start + block].astype(F32)
            for source in range(1, count):
                total = total + land_ref[source, :, start : start + block].astype(F32)
            out_ref[:, start : start + block] = total.astype(out_ref.dtype)


def exchange(values, axis, number, name, gather=False, reduce=None):
    count = lax.axis_size(axis)
    block = values.shape if gather else values.shape[1:]
    landing = (count,) + block
    semaphores = [
        pltpu.SemaphoreType.DMA((count,)),
        pltpu.SemaphoreType.DMA((count,)),
        pltpu.SemaphoreType.DMA,
    ]
    if reduce is None:
        result = jax.ShapeDtypeStruct(landing, values.dtype)
        scratch = semaphores
    else:
        result = jax.ShapeDtypeStruct(block, reduce)
        scratch = [pltpu.VMEM(landing, values.dtype)] + semaphores
    return pl.pallas_call(
        functools.partial(exchange_kernel, axis, count, gather, reduce is not None),
        out_shape=result,
        in_specs=[vmem()],
        out_specs=vmem(),
        scratch_shapes=scratch,
        compiler_params=pltpu.CompilerParams(collective_id=number, has_side_effects=True),
        cost_estimate=pl.CostEstimate(flops=0, bytes_accessed=200_000_000, transcendentals=0),
        name=name,
    )(values)


def prologue_kernel(
    ring, count, token_ref, weight_ref, tokens_out, weights_out,
    token_send, token_recv, right_send, right_recv, left_send, left_recv,
    pair_send, pair_recv, own_sem,
):
    me = lax.axis_index("fsdp")
    row = lax.axis_index("dp")
    chip, core = row // 2, lax.rem(row, 2)

    def place(step):
        return lax.rem(chip + step, ring) * 2 + core

    partner = {"dp": chip * 2 + (1 - core)}
    after = {"dp": place(1)}
    before = {"dp": place(ring - 1)}
    peers = [{"fsdp": lax.rem(me + step, count)} for step in range(1, count)]
    barrier = pltpu.get_barrier_semaphore()
    for device in peers + [partner, after, before]:
        pl.semaphore_signal(
            barrier, inc=1, device_id=device, device_id_type=pl.DeviceIdType.MESH
        )
    pl.semaphore_wait(barrier, count + 2)

    def send(src, dst, send_sem, recv_sem, device):
        copy = pltpu.make_async_remote_copy(
            src_ref=src,
            dst_ref=dst,
            send_sem=send_sem,
            recv_sem=recv_sem,
            device_id=device,
            device_id_type=pl.DeviceIdType.MESH,
        )
        copy.start()
        return copy

    def slot(step):
        return weights_out.at[:, place(step)]

    rights = ring // 2
    lefts = ring - 1 - rights
    right = send(weight_ref, slot(0), right_send.at[0], right_recv.at[0], after)
    left = send(weight_ref, slot(0), left_send.at[0], left_recv.at[0], before)
    tail = [send(weight_ref, slot(0), pair_send.at[0], pair_recv.at[0], partner)]
    for step, device in enumerate(peers):
        tail.append(
            send(token_ref, tokens_out.at[me], token_send.at[step], token_recv.at[step], device)
        )
    own = [
        pltpu.make_async_copy(weight_ref, slot(0), own_sem.at[0]),
        pltpu.make_async_copy(token_ref, tokens_out.at[me], own_sem.at[1]),
    ]
    for copy in own:
        copy.start()
    for s in range(1, rights + 1):
        right.wait()
        block = slot(ring - s)
        if s < rights:
            right = send(block, block, right_send.at[s], right_recv.at[s], after)
        tail.append(send(block, block, pair_send.at[s], pair_recv.at[s], partner))
        if s <= lefts:
            left.wait()
            block = slot(s)
            if s < lefts:
                left = send(block, block, left_send.at[s], left_recv.at[s], before)
            tail.append(
                send(block, block, pair_send.at[rights + s], pair_recv.at[rights + s], partner)
            )
    for copy in own + tail:
        copy.wait()


def prologue(tokens, weights, number):
    rows_count = lax.axis_size("dp")
    count = lax.axis_size("fsdp")
    ring = rows_count // 2
    parts, depth, width = weights.shape
    return pl.pallas_call(
        functools.partial(prologue_kernel, ring, count),
        out_shape=(
            jax.ShapeDtypeStruct((count,) + tokens.shape, tokens.dtype),
            jax.ShapeDtypeStruct((parts, rows_count, depth, width), weights.dtype),
        ),
        in_specs=[vmem()] * 2,
        out_specs=(vmem(), vmem()),
        scratch_shapes=[
            pltpu.SemaphoreType.DMA((count - 1,)),
            pltpu.SemaphoreType.DMA((count - 1,)),
            pltpu.SemaphoreType.DMA((ring,)),
            pltpu.SemaphoreType.DMA((ring,)),
            pltpu.SemaphoreType.DMA((ring,)),
            pltpu.SemaphoreType.DMA((ring,)),
            pltpu.SemaphoreType.DMA((ring,)),
            pltpu.SemaphoreType.DMA((ring,)),
            pltpu.SemaphoreType.DMA((2,)),
        ],
        compiler_params=pltpu.CompilerParams(collective_id=number, has_side_effects=True),
        name="prologue",
    )(tokens, weights)


def hidden_kernel(token_ref, gate_own, gate_other, up_own, gate_ref, up_ref):
    half = gate_own.shape[0]
    own = token_ref[:, :half]
    other = token_ref[:, half:]
    gate = jnp.dot(own, gate_own[...], preferred_element_type=F32)
    gate = gate + jnp.dot(other, gate_other[...], preferred_element_type=F32)
    gate_ref[...] = gate / (1.0 + jnp.exp(-gate))
    up_ref[...] = jnp.dot(own, up_own[...], preferred_element_type=F32)


def down_kernel(token_ref, gate_ref, up_ref, up_other, down_own, down_other, out_ref):
    half = up_other.shape[0]
    up = up_ref[...] + jnp.dot(
        token_ref[:, half:], up_other[...], preferred_element_type=F32
    )
    activation = (gate_ref[...] * up).astype(BF16)
    out_ref[:, :half] = dot_t(activation, down_own[...]).astype(BF16)
    out_ref[:, half:] = dot_t(activation, down_other[...]).astype(BF16)


def experts(tokens, gates, ups, downs):
    count, width = tokens.shape
    depth, units = gates[0].shape
    part = jax.ShapeDtypeStruct((count, units), F32)
    params = pltpu.CompilerParams(vmem_limit_bytes=40 * 1024 * 1024)
    gate, up = pl.pallas_call(
        hidden_kernel,
        out_shape=(part, part),
        in_specs=[vmem()] * 4,
        out_specs=(vmem(), vmem()),
        compiler_params=params,
        cost_estimate=pl.CostEstimate(
            flops=6 * count * depth * units, bytes_accessed=30_000_000, transcendentals=0
        ),
        name="experts_hidden",
    )(tokens, gates[0], gates[1], ups[0])
    return pl.pallas_call(
        down_kernel,
        out_shape=jax.ShapeDtypeStruct((count, width), BF16),
        in_specs=[vmem()] * 6,
        out_specs=vmem(),
        compiler_params=params,
        name="experts_down",
    )(tokens, gate, up, ups[1], downs[0], downs[1])


def torus_ids(axis, side):
    me = lax.axis_index(axis)
    y, x = me // side, lax.rem(me, side)

    def peer(along_y, step):
        if along_y:
            return {axis: lax.rem(y + step, side) * side + x}
        return {axis: y * side + lax.rem(x + step, side)}

    return y, x, peer


def torus_barrier(peer, side):
    barrier = pltpu.get_barrier_semaphore()
    for along_y in (False, True):
        for step in range(1, side):
            pl.semaphore_signal(
                barrier,
                inc=1,
                device_id=peer(along_y, step),
                device_id_type=pl.DeviceIdType.MESH,
            )
    pl.semaphore_wait(barrier, 2 * (side - 1))


def torus_gather_kernel(axis, side, src_ref, out_ref, send_sem, recv_sem, own_sem):
    y, x, peer = torus_ids(axis, side)
    half = src_ref.shape[0] // 2
    rows = [pl.ds(0, half), pl.ds(half, half)]
    part = [pl.ds(0, side // 2), pl.ds(side // 2, side - side // 2)]
    torus_barrier(peer, side)

    def send(h, number, src, dst, device):
        copy = pltpu.make_async_remote_copy(
            src_ref=src,
            dst_ref=dst,
            send_sem=send_sem.at[h, number],
            recv_sem=recv_sem.at[h, number],
            device_id=device,
            device_id_type=pl.DeviceIdType.MESH,
        )
        copy.start()
        return copy

    first = [
        [
            send(h, step - 1, src_ref.at[rows[h]], out_ref.at[y, x, rows[h]], peer(h == 1, step))
            for step in range(1, side)
        ]
        for h in range(2)
    ]
    own = pltpu.make_async_copy(src_ref, out_ref.at[y, x], own_sem)
    own.start()
    own.wait()

    def group(h, step, blocks):
        if h == 0:
            return out_ref.at[lax.rem(y + step, side), blocks, rows[h]]
        return out_ref.at[blocks, lax.rem(x + step, side), rows[h]]

    whole = pl.ds(0, side)
    second = []
    for h in range(2):
        for copy in first[h]:
            copy.wait()
        second.append(
            [
                send(h, 3, group(h, 0, whole), group(h, 0, whole), peer(h == 0, 1)),
                send(h, 4, group(h, 0, whole), group(h, 0, whole), peer(h == 0, side - 1)),
            ]
        )
    third = []
    for h in range(2):
        for k, back in ((0, side - 1), (1, 1)):
            second[h][k].wait()
            source = group(h, back, part[k])
            third.append(send(h, 5 + k, source, source, peer(h == 0, side - back)))
    for copy in third:
        copy.wait()


def torus_gather(values, axis, number, name):
    count = lax.axis_size(axis)
    side = 4
    return pl.pallas_call(
        functools.partial(torus_gather_kernel, axis, side),
        out_shape=jax.ShapeDtypeStruct((side, count // side) + values.shape, values.dtype),
        in_specs=[vmem()],
        out_specs=vmem(),
        scratch_shapes=[
            pltpu.SemaphoreType.DMA((2, 7)),
            pltpu.SemaphoreType.DMA((2, 7)),
            pltpu.SemaphoreType.DMA,
        ],
        compiler_params=pltpu.CompilerParams(collective_id=number, has_side_effects=True),
        cost_estimate=pl.CostEstimate(flops=0, bytes_accessed=60_000_000, transcendentals=0),
        name=name,
    )(values)


def torus_sum_kernel(
    axis, side, src_ref, out_ref, land_ref, relay_ref, sum_ref, last_ref, send_sem, recv_sem
):
    y, x, peer = torus_ids(axis, side)
    half = src_ref.shape[2] // 2
    width = src_ref.shape[3]
    block = width // 3
    rows = [pl.ds(0, half), pl.ds(half, half)]
    part = [pl.ds(0, side // 2), pl.ds(side // 2, side - side // 2)]
    whole = pl.ds(0, side)
    torus_barrier(peer, side)

    def send(h, number, src, dst, device):
        copy = pltpu.make_async_remote_copy(
            src_ref=src,
            dst_ref=dst,
            send_sem=send_sem.at[h, number],
            recv_sem=recv_sem.at[h, number],
            device_id=device,
            device_id_type=pl.DeviceIdType.MESH,
        )
        copy.start()
        return copy

    def terms(h, step, blocks):
        if h == 0:
            return src_ref.at[blocks, lax.rem(x + step, side), rows[h]]
        return src_ref.at[lax.rem(y + step, side), blocks, rows[h]]

    far, near, relays = [], [], []
    for h in range(2):
        far.append(
            [
                send(h, 0, terms(h, 2, part[0]), relay_ref.at[h, 0], peer(h == 1, 1)),
                send(h, 1, terms(h, 2, part[1]), relay_ref.at[h, 1], peer(h == 1, side - 1)),
            ]
        )
    for h in range(2):
        near.append(
            [
                send(h, 2, terms(h, 1, whole), land_ref.at[h, 0], peer(h == 1, 1)),
                send(h, 3, terms(h, side - 1, whole), land_ref.at[h, 2], peer(h == 1, side - 1)),
            ]
        )
    for h in range(2):
        for k, step in ((0, 1), (1, side - 1)):
            far[h][k].wait()
            relays.append(
                send(
                    h, 4 + k, relay_ref.at[h, k], land_ref.at[h, 1, part[k]], peer(h == 1, step)
                )
            )
    for h in range(2):
        for copy in near[h]:
            copy.wait()
    for copy in relays:
        copy.wait()
    last = []
    for h in range(2):
        for b in range(side):
            for start in range(0, width, block):
                cols = slice(start, start + block)
                if h == 0:
                    total = src_ref[b, x, 0:half, cols].astype(F32)
                else:
                    total = src_ref[y, b, half : 2 * half, cols].astype(F32)
                for k in range(side - 1):
                    total = total + land_ref[h, k, b, :, cols].astype(F32)
                sum_ref[h, b, :, cols] = total.astype(sum_ref.dtype)
        mine = y if h == 0 else x
        for step in range(1, side):
            last.append(
                send(
                    h,
                    5 + step,
                    sum_ref.at[h, lax.rem(mine + step, side)],
                    last_ref.at[h, step - 1],
                    peer(h == 0, step),
                )
            )
    for copy in last:
        copy.wait()
    for h in range(2):
        mine = y if h == 0 else x
        for start in range(0, width, block):
            cols = slice(start, start + block)
            total = sum_ref[h, mine, :, cols].astype(F32)
            for k in range(side - 1):
                total = total + last_ref[h, k, :, cols].astype(F32)
            out_ref[h * half : (h + 1) * half, cols] = total.astype(out_ref.dtype)


def torus_sum(values, axis, number, name):
    count, rows, width = values.shape
    side = 4
    half = rows // 2
    return pl.pallas_call(
        functools.partial(torus_sum_kernel, axis, side),
        out_shape=jax.ShapeDtypeStruct((rows, width), values.dtype),
        in_specs=[vmem()],
        out_specs=vmem(),
        scratch_shapes=[
            pltpu.VMEM((2, side - 1, side, half, width), values.dtype),
            pltpu.VMEM((2, 2, side // 2, half, width), values.dtype),
            pltpu.VMEM((2, side, half, width), values.dtype),
            pltpu.VMEM((2, side - 1, half, width), values.dtype),
            pltpu.SemaphoreType.DMA((2, 9)),
            pltpu.SemaphoreType.DMA((2, 9)),
        ],
        compiler_params=pltpu.CompilerParams(
            collective_id=number, has_side_effects=True, vmem_limit_bytes=40 * 1024 * 1024
        ),
        name=name,
    )(values.reshape(side, count // side, rows, width))


def local(
    hidden_in,
    cache_pool,
    project_in,
    project_out,
    norm_first,
    norm_second,
    router,
    gate_up,
    expert_down,
    lengths,
    prompt_pages,
    own_pages,
    groups,
    move_target,
    routes,
):
    rows_count = lax.axis_size("dp")
    fsdp_count = lax.axis_size("fsdp")
    my_row = lax.axis_index("dp")
    my_column = lax.axis_index("fsdp")
    req_local, model_width = hidden_in.shape
    req_row = req_local * fsdp_count
    movers = move_target.shape[1]
    staying = req_row - movers
    pages, page_len = cache_pool.shape[:2]
    head_cols = cache_pool.shape[3]
    expert_count = router.shape[1]
    rows_per_expert = rows_count // expert_count
    slots_row = (CAP + rows_per_expert - 1) // rows_per_expert
    units_here = gate_up.shape[3]
    features_here = gate_up.shape[1]

    same_core = [list(range(k, rows_count, rows_per_expert)) for k in range(rows_per_expert)]

    def spread_weights(values):
        return lax.all_to_all(
            values, "dp", split_axis=0, concat_axis=0, tiled=True, axis_index_groups=same_core
        )

    weights = jnp.concatenate(
        [jnp.transpose(project_in, (1, 0, 2)), project_out.T[None]], axis=0
    )
    row_tokens, weights = prologue(hidden_in, weights, 0)
    row_tokens = row_tokens.reshape(req_row, model_width)
    weights = weights.reshape(weights.shape[0], model_width, head_cols)
    weight_out = weights[3]
    units_wide = -(-units_here // 128) * 128

    def widen(values):
        return jnp.pad(values, ((0, 0), (0, 0), (0, units_wide - units_here)))

    gate_cols = widen(gate_up[:, :, 0])
    expert_down = widen(expert_down)
    expert_down, weights, gate_cols = lax.optimization_barrier((expert_down, weights, gate_cols))
    swap = [(d, d ^ 1) for d in range(rows_count)]
    down_own = spread_weights(expert_down)

    group_hit = (
        groups[:, None] == jnp.arange(prompt_pages.shape[0], dtype=jnp.int32)[None, :]
    ).astype(jnp.int32)
    prompt_list = jnp.sum(group_hit[:, :, None] * prompt_pages[None, :, :], axis=1)
    page_list = jnp.concatenate([prompt_list, own_pages], axis=1)
    position = lax.dynamic_slice_in_dim(lengths, my_row * req_row, req_row)
    page_numbers = jnp.arange(pages, dtype=jnp.int32)
    limit = jnp.zeros((req_row, pages), jnp.int32)
    for j in range(page_list.shape[1]):
        valid = jnp.clip(position - page_len * j, 0, page_len)
        limit += jnp.where(page_list[:, j : j + 1] == page_numbers[None, :], valid[:, None], 0)

    heads_out = attention(row_tokens, norm_first, weights, position, limit, cache_pool)

    row_numbers = jnp.arange(rows_count, dtype=jnp.int32)
    send_select = (move_target[my_row][None, :] == row_numbers[:, None]).astype(BF16)
    leaving = jnp.concatenate([heads_out[staying:], row_tokens[staying:]], axis=1)
    leaving_send = jnp.dot(send_select, leaving, preferred_element_type=F32).astype(BF16)
    leaving_send, down_own = lax.optimization_barrier((leaving_send, down_own))
    down_own = down_own.reshape(-1, units_wide)
    leaving_recv = exchange(leaving_send[:, None, :], "dp", 1, "leaving")[:, 0]
    leaving_recv, gate_cols = lax.optimization_barrier((leaving_recv, gate_cols))
    down_other = lax.ppermute(down_own, "dp", swap)
    gate_own = spread_weights(gate_cols)
    arrive_select = (move_target == my_row).astype(BF16)
    arrived = lax.dot_general(
        arrive_select, leaving_recv, (((0,), (0,)), ((), ())), preferred_element_type=F32
    ).astype(BF16)
    heads_row = jnp.concatenate([heads_out[:staying], arrived[:, :head_cols]], axis=0)
    mine_tokens = jnp.where(
        my_column == fsdp_count - 1, arrived[:, head_cols:], hidden_in
    )
    partial_out = dot_t(heads_row, weight_out).astype(BF16)
    attn_proj = exchange(
        partial_out.reshape(fsdp_count, req_local, model_width),
        "fsdp",
        2,
        "partial_out",
        reduce=F32,
    )
    attn_proj, gate_up = lax.optimization_barrier((attn_proj, gate_up))
    up_cols = widen(gate_up[:, :, 1])
    resid = mine_tokens.astype(F32) + attn_proj
    moe_in = rms_scale(resid, norm_second).astype(BF16)
    moe_in, gate_own, up_cols = lax.optimization_barrier((moe_in, gate_own, up_cols))
    logits = jnp.dot(moe_in, router, preferred_element_type=F32)
    expert_ids = jnp.arange(expert_count, dtype=jnp.int32)
    picked = routes[:, :, None] == expert_ids[None, None, :]
    chosen = jnp.sum(jnp.where(picked, logits[:, None, :], 0.0), axis=-1)
    weight_pair = jnp.stack(
        [jax.nn.sigmoid(chosen[:, 0] - chosen[:, 1]), jax.nn.sigmoid(chosen[:, 1] - chosen[:, 0])],
        axis=1,
    )
    mix_expert = jnp.sum(picked.astype(F32) * weight_pair[:, :, None], axis=1)
    member = jnp.sum(picked.astype(jnp.int32), axis=1)
    rank_expert = jnp.cumsum(member, axis=0) - member
    expert_of_row = (row_numbers[:, None] // rows_per_expert == expert_ids[None, :]).astype(
        jnp.int32
    )
    replica_of_row = row_numbers % rows_per_expert
    member_row = jnp.sum(member[:, None, :] * expert_of_row[None, :, :], axis=-1)
    rank_row = jnp.sum(rank_expert[:, None, :] * expert_of_row[None, :, :], axis=-1)
    mix_row = jnp.sum(mix_expert[:, None, :] * expert_of_row[None, :, :].astype(F32), axis=-1)
    slot_ids = jnp.arange(slots_row, dtype=jnp.int32)
    wanted_rank = slot_ids[None, :, None] * rows_per_expert + replica_of_row[:, None, None]
    select = (member_row.T[:, None, :] == 1) & (rank_row.T[:, None, :] == wanted_rank)
    dispatch = jnp.einsum(
        "dst,tm->dsm", select.astype(BF16), moe_in, preferred_element_type=F32
    ).astype(BF16)
    by_core = dispatch.reshape(rows_count // 2, 2, slots_row, rows_count // 2, 2, features_here)
    half = model_width // 2
    cores = [by_core[:, :, :, :, c].reshape(rows_count // 2, 2, slots_row, half) for c in range(2)]
    dispatch = jnp.stack(
        [
            jnp.concatenate([cores[0][:, 0], cores[1][:, 0]], axis=-1),
            jnp.concatenate([cores[1][:, 1], cores[0][:, 1]], axis=-1),
        ],
        axis=1,
    ).reshape(rows_count, slots_row, model_width)
    gate_own = gate_own.reshape(-1, units_wide)
    received = exchange(dispatch, "dp", 3, "dispatch")
    received, up_cols = lax.optimization_barrier((received, up_cols))
    gate_other = lax.ppermute(gate_own, "dp", swap)
    up_own = spread_weights(up_cols).reshape(-1, units_wide)
    expert_tokens = torus_gather(
        received.reshape(rows_count * slots_row, model_width), "fsdp", 4, "expert_tokens"
    )
    expert_tokens, up_own = lax.optimization_barrier((expert_tokens, up_own))
    up_other = lax.ppermute(up_own, "dp", swap)
    flattened = expert_tokens.reshape(-1, model_width)
    expert_y = experts(
        flattened, (gate_own, gate_other), (up_own, up_other), (down_own, down_other)
    )
    returned = torus_sum(
        expert_y.reshape(fsdp_count, rows_count * slots_row, model_width),
        "fsdp",
        5,
        "expert_sums",
    )
    back_rows = exchange(
        returned.reshape(rows_count, slots_row, model_width), "dp", 6, "back_rows"
    )
    coefficient = select.astype(F32) * mix_row.T[:, None, :]
    coefficient = coefficient.reshape(rows_count // 2, 2, slots_row, req_local)
    back_rows = back_rows.astype(F32).reshape(rows_count // 2, 2, slots_row, model_width)
    sums = [
        jnp.einsum(
            "dst,dsm->tm", coefficient[:, c], back_rows[:, c], precision=lax.Precision.HIGHEST
        )
        for c in range(2)
    ]
    by_core = [
        sums[0][:, :half] + sums[1][:, half:],
        sums[0][:, half:] + sums[1][:, :half],
    ]
    moe_total = jnp.stack(
        [part.reshape(req_local, rows_count // 2, features_here) for part in by_core], axis=2
    ).reshape(req_local, model_width)
    return (resid + moe_total).astype(BF16)


def solution(mesh):
    placed = (
        P(("dp", "fsdp"), None),
        P("dp", None, None, "fsdp"),
        P("dp", None, "fsdp"),
        P("fsdp", "dp"),
        P(),
        P(),
        P(),
        P(None, "dp", None, "fsdp"),
        P(None, "dp", "fsdp"),
        P(),
        P("dp", None),
        P("dp", None),
        P("dp"),
        P(),
        P(("dp", "fsdp"), None),
    )
    return jax.shard_map(
        local, mesh=mesh, in_specs=placed, out_specs=P(("dp", "fsdp"), None), check_vma=False
    )
```
